128 devices in a mesh: head: 4 (over z_lo, core), track: 32 (over y, z_hi, x).
Axes of the slice: x: 4, y: 4, z: 4 (z_hi: 2, z_lo: 2; z = z_hi * 2 + z_lo), core: 2. Of those that a mesh axis runs over, the one named last changes fastest.
Arguments:
- potential: float32 [256, 4096, 128], P('head', 'track'), may hold values from -6 to 6
- source: float32 [256, 4096, 128], P('head', 'track'), may hold values from -6 to 6
- depth_kernel: float32 [3, 128], replicated, may hold values from -0.5 to 0.5
- magnet: float32 [3, 32, 16384], P(None, 'track', 'head'), may hold values from -0.8 to 0.8
- footprint: int32 [32, 16384], P('track', 'head'), may hold values from 0 to 262143, as said below
- temp_index: int32 [32, 16384], P('track', 'head'), may hold values from 0 to 127
- temp_profile: float32 [128], replicated, may hold values from 0.3 to 1.4
- self_tiles: float32 [32, 128, 128, 128], P('track', 'head'), may hold values from -0.5 to 0.5
- next_tiles: float32 [32, 128, 128, 128], P('track', 'head'), may hold values from -0.5 to 0.5
Outputs:
- relaxed: float32 [256, 4096, 128], P('head', 'track')
- magnet_out: float32 [3, 32, 16384], P(None, 'track', 'head')
The draws below stay inside these ranges and needn't reach their ends.
Inputs may be any that keep to these rules, and one draw needn't show every extreme that they name: Within the 4096 grains of one device (an aligned block of a track tile), no more than 256 have footprint cells in any one pole block of 8192 cells; in every draw one pole block, the same for every device, takes exactly 256 grains of every device.
All inputs are finite; a program needn't handle non-finite values.
Results may differ from the reference program's by a relative error of at most 0.0001.
Values sent between devices are 32-bit elements; how exact they have to be, the bound alone decides.
A program may use at most 320 MiB of HBM per device.

```python
import jax
import jax.numpy as jnp
from jax import lax

HX = 64
HY = 128
HZ = 128
GRAIN_DEV = 4096
TILE = 128
NTEMP = 128
NX = 256
NY = 4096
GRAINS_TRACK = 16384
TILES_TRACK = 128
SURFACE_ALL = 262144
CAP = 256
N_HEAD = 4
N_TRACK = 32


def draw_footprint(key, part):
    blocks = N_TRACK * N_HEAD
    key_hot, key_perm, key_step, key_cell = jax.random.split(key, 4)
    hot = jax.random.randint(key_hot, (), 0, N_TRACK, dtype=jnp.int32)
    perm_keys = jax.random.split(key_perm, blocks)
    orders = jax.vmap(lambda sub: jax.random.permutation(sub, GRAIN_DEV))(perm_keys).astype(jnp.int32)
    ranks = jnp.argsort(orders, axis=1, stable=True).astype(jnp.int32)
    rest = ranks - CAP
    step_add = jax.random.randint(key_step, (blocks, GRAIN_DEV), 0, 2, dtype=jnp.int32)
    other = (rest + step_add) % (N_TRACK - 1)
    other = other + (other >= hot).astype(jnp.int32)
    owner = jnp.where(ranks < CAP, hot, other)
    offset = jax.random.randint(key_cell, (blocks, GRAIN_DEV), 0, HX * HY, dtype=jnp.int32)
    cells = owner * (HX * HY) + offset
    return cells.reshape(N_TRACK, N_HEAD * GRAIN_DEV).astype(jnp.int32)


def plant(array, key, least, high):
    dims = array.shape
    index_at = [jax.random.randint(jax.random.fold_in(key, axis), (), 0, dims[axis]) for axis in range(len(dims))]
    array = array.at[tuple(index_at)].set(least)
    longest = dims.index(max(dims))
    index_at[longest] = (index_at[longest] + 1) % dims[longest]
    return array.at[tuple(index_at)].set(high)


def block_levels(rng, extent, cuts, smallest, high):
    level = 1.0
    for dim, blocks in cuts:
        heights = jax.random.uniform(jax.random.fold_in(jax.random.fold_in(rng, 6), dim), (blocks,), jnp.float32, smallest / len(cuts), high / len(cuts))
        level = level * jnp.repeat(jnp.exp(heights), extent[dim] // blocks).reshape((-1,) + (1,) * (len(extent) - 1 - dim))
    return level


def bell_draw(stream_key, dims, spread, limit, shards=(), kind=jnp.bfloat16):
    drawn = jax.random.normal(stream_key, dims, jnp.float32) * spread
    if len(shards) > 0:
        drawn = block_levels(stream_key, dims, shards, -0.22, 0.18) * drawn
    return jnp.clip(drawn, min=-limit, max=limit).astype(kind)


def setup_inputs(seed: int = 0) -> dict:
    key_list = jax.random.split(jax.random.key(seed), 10)
    potential = bell_draw(key_list[0], (NX, NY, HZ), 1.0, 6.0, ((0, 4), (1, 32)), jnp.float32)
    source = bell_draw(key_list[1], (NX, NY, HZ), 1.0, 6.0, ((0, 4), (1, 32)), jnp.float32)
    depth_kernel = bell_draw(key_list[2], (3, HZ), HZ ** -0.5, 0.5, (), jnp.float32)
    magnet = jnp.clip(jax.random.uniform(key_list[3], (3, N_TRACK, GRAINS_TRACK), jnp.float32, -0.8, 0.8) * block_levels(key_list[3], (3, N_TRACK, GRAINS_TRACK), ((1, 32), (2, 4)), -0.4, 0.0), -0.8, 0.8)
    footprint = draw_footprint(jax.random.fold_in(key_list[9], 71), 0)
    temp_index = plant(jax.random.randint(key_list[5], (N_TRACK, GRAINS_TRACK), 0, NTEMP), jax.random.fold_in(key_list[5], 1), 0, NTEMP - 1).astype(jnp.int32)
    temp_profile = jnp.clip(jax.random.uniform(key_list[6], (NTEMP,), jnp.float32, 0.3, 1.4), 0.3, 1.4)
    self_tiles = bell_draw(key_list[7], (N_TRACK, TILES_TRACK, TILE, TILE), TILE ** -0.5, 0.5, ((0, 32), (1, 4)), jnp.float32)
    next_tiles = bell_draw(key_list[8], (N_TRACK, TILES_TRACK, TILE, TILE), TILE ** -0.5, 0.5, ((0, 32), (1, 4)), jnp.float32)
    return dict(potential=potential, source=source, depth_kernel=depth_kernel, magnet=magnet, footprint=footprint, temp_index=temp_index, temp_profile=temp_profile, self_tiles=self_tiles, next_tiles=next_tiles)


HIGH = lax.Precision.HIGHEST


def relax_sweep(padded, source):
    center = padded[1:-1, 1:-1]
    deep = jnp.pad(center, ((0, 0), (0, 0), (1, 1)))
    others = [padded[2:, 1:-1], padded[:-2, 1:-1], padded[1:-1, 2:], padded[1:-1, :-2], deep[:, :, 2:], deep[:, :, :-2]]
    numer = source
    denom = jnp.ones_like(center)
    for other in others:
        differ = other - center
        perm = 1.0 + 4.0 / (1.0 + 4.0 * differ * differ)
        numer = numer + perm * differ
        denom = denom + perm
    return center + 0.8 * numer / denom


def cross_comp(a_vec, b_vec):
    return jnp.stack([a_vec[1] * b_vec[2] - a_vec[2] * b_vec[1], a_vec[2] * b_vec[0] - a_vec[0] * b_vec[2], a_vec[0] * b_vec[1] - a_vec[1] * b_vec[0]])


def llb_section(state, field, target):
    sq_norm = jnp.sum(state * state, axis=0)
    total = field + 0.5 * (1.0 - sq_norm / target) * state
    turn = cross_comp(state, total)
    damp = cross_comp(state, turn)
    along = jnp.sum(state * total, axis=0)
    return state + 0.1 * (-turn - 0.5 * damp + 0.3 * along * state)


def reference(potential, source, depth_kernel, magnet, footprint, temp_index, temp_profile, self_tiles, next_tiles):
    n_head = NX // HX
    n_track = NY // HY
    relaxed = potential
    for sweep_idx in range(2):
        padded = jnp.pad(relaxed, ((1, 1), (1, 1), (0, 0)))
        relaxed = relax_sweep(padded, source)
    surface = jnp.einsum('kz,xyz->kxy', depth_kernel, relaxed, precision=HIGH)
    table = surface.reshape(3, n_head, HX, n_track, HY).transpose(0, 1, 3, 2, 4).reshape(3, n_head, SURFACE_ALL)
    row_block = (jnp.arange(GRAINS_TRACK, dtype=jnp.int32) // GRAIN_DEV).astype(jnp.int32)
    row_block = jnp.broadcast_to(row_block[None, :], footprint.shape)
    applied = table[:, row_block, footprint]
    temp = temp_profile[temp_index]
    target = 0.05 + jnp.maximum(1.0 - temp, 0.0)
    state = magnet
    for section in range(2):
        tiles = state.reshape(3, n_track, TILES_TRACK, TILE)
        padded = jnp.pad(tiles, ((0, 0), (0, 0), (1, 1), (0, 0)))
        ex = jnp.einsum('tkij,ctkj->ctki', self_tiles, padded[:, :, 1:-1], precision=HIGH)
        ex = ex + jnp.einsum('tkij,ctkj->ctki', next_tiles, padded[:, :, :-2], precision=HIGH)
        ex = ex + jnp.einsum('tkji,ctkj->ctki', next_tiles, padded[:, :, 2:], precision=HIGH)
        ex = ex.reshape(3, n_track, GRAINS_TRACK)
        state = llb_section(state, applied + ex, target)
    return relaxed, state
```

```python
import functools

import jax
import jax.numpy as jnp
from jax import lax
from jax.experimental import pallas as pl
from jax.experimental.pallas import tpu as pltpu
from jax.sharding import PartitionSpec as P

F32 = jnp.float32
BF16 = jnp.bfloat16
I32 = jnp.int32
NN = (((1,), (0,)), ((), ()))
NT = (((1,), (1,)), ((), ()))
ROW0 = 8


def mxu(a, b, dims):
    return lax.dot_general(a, b, dims, preferred_element_type=F32)


def split(a):
    high = a.astype(BF16)
    return high, (a - high.astype(F32)).astype(BF16)


def face(a, b):
    differ = b - a
    perm = 1.0 + pltpu.reciprocal(0.25 + differ * differ)
    return perm, perm * differ


def relax_rows(lower, center, upper, before, after, drive, carried, first, last):
    perm, flux = face(center, upper)
    numer = (drive - carried[1]) + flux
    denom = (1.0 + carried[0]) + perm
    carried = (perm, flux)
    perm, flux = face(before, center)
    numer = numer - flux
    denom = denom + perm
    depth = center.shape[1]
    for other in (
        after,
        jnp.where(last, 0.0, pltpu.roll(center, depth - 1, 1)),
        jnp.where(first, 0.0, pltpu.roll(center, 1, 1)),
    ):
        perm, flux = face(center, other)
        numer = numer + flux
        denom = denom + perm
    return center + (0.8 * numer) * pltpu.reciprocal(denom), carried


def one_hot_rows(index, count):
    lanes = index.shape[1]
    rows = lax.broadcasted_iota(I32, (count, lanes), 0)
    return jnp.where(rows == jnp.broadcast_to(index, (count, lanes)), 1.0, 0.0)


def lookup(table, address):
    hot = jnp.concatenate([one_hot_rows(a & 127, 128) for a in address], axis=1).astype(BF16)
    found = mxu(table, jnp.concatenate([hot, hot], axis=0), NN)
    results = []
    for part, a in enumerate(address):
        group = jnp.broadcast_to(a >> 8, (8, 128))
        odd = jnp.broadcast_to((a >> 7) & 1, (8, 128))
        total = jnp.zeros((8, 128), F32)
        for g in range(table.shape[0] // 8):
            total = total + jnp.where(
                group == g, found[8 * g : 8 * g + 8, 128 * part : 128 * part + 128], 0.0
            )
        results.append(jnp.where(odd == 0, total, pltpu.roll(total, 7, 0)))
    return results


def halves(rows):
    high, low = split(rows)
    return jnp.concatenate([high, low], axis=1)


def llb_section(state, field, target):
    mx, my, mz = state
    sq_norm = mx * mx + my * my + mz * mz
    pull = 0.5 * (1.0 - sq_norm / target)
    hx, hy, hz = (f + pull * m for f, m in zip(field, state))
    tx, ty, tz = my * hz - mz * hy, mz * hx - mx * hz, mx * hy - my * hx
    dx, dy, dz = my * tz - mz * ty, mz * tx - mx * tz, mx * ty - my * tx
    along = 0.3 * (mx * hx + my * hy + mz * hz)
    return tuple(
        m + 0.1 * (along * m - t - 0.5 * d)
        for m, t, d in zip(state, (tx, ty, tz), (dx, dy, dz))
    )


def kernel(
    n_head,
    n_track,
    pot_hbm,
    src_hbm,
    dk_hbm,
    mag_hbm,
    foot_hbm,
    temp_hbm,
    prof_hbm,
    self_hbm,
    next_hbm,
    out_hbm,
    mout_hbm,
    pot,
    mid,
    src,
    dk,
    mag,
    foot,
    tidx,
    prof,
    tself,
    tnext,
    self_high,
    self_low,
    next_high,
    next_low,
    lhs,
    ex,
    rim,
    rim_new,
    edge,
    addr,
    ask,
    asked,
    surf,
    answer,
    answered,
    field,
    in_sem,
    out_sem,
    halo_send,
    halo_recv,
    mid_send,
    mid_recv,
    rim_send,
    rim_recv,
    ask_send,
    ask_recv,
    ans_send,
    ans_recv,
):
    head = lax.axis_index("head")
    track = lax.axis_index("track")
    n_x, n_y = src.shape[0], src.shape[1]
    n_tiles = mag.shape[1]
    inner = pl.ds(ROW0, n_y)

    has_low_x, has_high_x = head > 0, head < n_head - 1
    has_low_y, has_high_y = track > 0, track < n_track - 1
    low_x, high_x = (head - 1, track), (head + 1, track)
    low_y, high_y = (head, track - 1), (head, track + 1)

    def partner(step):
        return lax.rem(track + step, n_track)

    loads = [
        pltpu.make_async_copy(a, b, in_sem.at[i])
        for i, (a, b) in enumerate(
            [
                (foot_hbm, foot),
                (pot_hbm, pot.at[pl.ds(1, n_x), inner, :]),
                (src_hbm, src),
                (mag_hbm, mag),
                (dk_hbm, dk),
                (temp_hbm, tidx),
                (prof_hbm, prof),
                (self_hbm, tself),
                (next_hbm, tnext),
            ]
        )
    ]
    for copy in loads:
        copy.start()

    for ref in (pot, mid):
        for plane in (0, n_x + 1):
            ref[plane, ROW0 : ROW0 + n_y, :] = jnp.zeros((n_y, ref.shape[2]), F32)
        for row in (ROW0 - 1, ROW0 + n_y):
            ref[1 : n_x + 1, row : row + 1, :] = jnp.zeros((n_x, 1, ref.shape[2]), F32)
    rim[...] = jnp.zeros(rim.shape, F32)
    rim_new[...] = jnp.zeros(rim_new.shape, F32)

    barrier = pltpu.get_barrier_semaphore()

    def greet(step, _):
        pl.semaphore_signal(barrier, inc=1, device_id=(head, partner(step)), device_id_type=pl.DeviceIdType.MESH)
        return 0

    lax.fori_loop(1, n_track, greet, 0)
    for there, device in ((has_low_x, low_x), (has_high_x, high_x)):

        @pl.when(there)
        def _():
            pl.semaphore_signal(barrier, inc=1, device_id=device, device_id_type=pl.DeviceIdType.MESH)

    n_greeted = n_track - 1 + has_low_x.astype(I32) + has_high_x.astype(I32)
    pl.semaphore_wait(barrier, n_greeted)

    def remote(a, b, send, recv, device):
        return pltpu.make_async_remote_copy(
            src_ref=a, dst_ref=b, send_sem=send, recv_sem=recv, device_id=device,
            device_id_type=pl.DeviceIdType.MESH,
        )

    def brick_halo(source, first, row, target, send, recv):
        rows, planes = pl.ds(row, n_y), pl.ds(first, n_x)
        all_x = pl.ds(1, n_x)
        return [
            (has_low_x, remote(source.at[first, rows, :], target.at[n_x + 1, inner, :], send.at[0], recv.at[1], low_x)),
            (has_high_x, remote(source.at[first + n_x - 1, rows, :], target.at[0, inner, :], send.at[1], recv.at[0], high_x)),
            (has_low_y, remote(source.at[planes, pl.ds(row, 1), :], target.at[all_x, pl.ds(ROW0 + n_y, 1), :], send.at[2], recv.at[3], low_y)),
            (has_high_y, remote(source.at[planes, pl.ds(row + n_y - 1, 1), :], target.at[all_x, pl.ds(ROW0 - 1, 1), :], send.at[3], recv.at[2], high_y)),
        ]

    def brick_wait(source, first, row, target, send, recv):
        rows, planes = pl.ds(row, n_y), pl.ds(first, n_x)
        all_x = pl.ds(1, n_x)
        waits = [
            (has_low_x, remote(source.at[first, rows, :], target.at[0, inner, :], send.at[0], recv.at[0], low_x)),
            (has_high_x, remote(source.at[first, rows, :], target.at[n_x + 1, inner, :], send.at[1], recv.at[1], high_x)),
            (has_low_y, remote(source.at[planes, pl.ds(row, 1), :], target.at[all_x, pl.ds(ROW0 - 1, 1), :], send.at[2], recv.at[2], low_y)),
            (has_high_y, remote(source.at[planes, pl.ds(row, 1), :], target.at[all_x, pl.ds(ROW0 + n_y, 1), :], send.at[3], recv.at[3], high_y)),
        ]
        for there, copy in waits:

            @pl.when(there)
            def _():
                copy.wait_send()
                copy.wait_recv()

    def start(copies):
        for there, copy in copies:

            @pl.when(there)
            def _():
                copy.start()

    start(brick_halo(pot_hbm, 0, 0, pot, halo_send, halo_recv))
    loads[3].wait()

    def rim_copies(source, target, slot):
        return [
            (has_low_x, remote(source.at[0], target.at[1], rim_send.at[slot], rim_recv.at[slot + 1], low_x)),
            (has_high_x, remote(source.at[1], target.at[0], rim_send.at[slot + 1], rim_recv.at[slot], high_x)),
        ]

    def rim_wait(source, target, slot):
        for i, (there, device) in enumerate(((has_low_x, low_x), (has_high_x, high_x))):

            @pl.when(there)
            def _():
                copy = remote(source.at[i], target.at[i], rim_send.at[slot + i], rim_recv.at[slot + i], device)
                copy.wait_send()
                copy.wait_recv()

    def put_edges(slot, state):
        edge[slot] = jnp.zeros((2, 8, 128), F32)
        for comp, value in enumerate(state):
            edge[slot, 0, comp : comp + 1, :] = value[0:1, :]
            edge[slot, 1, comp : comp + 1, :] = value[n_tiles - 1 : n_tiles, :]

    state = [mag[comp] for comp in range(3)]
    put_edges(0, state)
    start(rim_copies(edge.at[0], rim, 0))

    loads[0].wait()
    later = lax.broadcasted_iota(I32, (128, 128), 0) < lax.broadcasted_iota(I32, (128, 128), 1)
    count_matrix = jnp.concatenate(
        [jnp.where(later, 1.0, 0.0), jnp.ones((128, 128), F32)], axis=1
    ).astype(BF16)
    before = jnp.zeros((n_track, 128), F32)
    asks = jnp.zeros((128, 128), F32)
    for chunk in range(n_tiles):
        cell = foot[chunk : chunk + 1, :]
        owner = cell >> 13
        hot = one_hot_rows(owner, n_track)
        counts = mxu(hot.astype(BF16), count_matrix, NN)
        place = jnp.sum(hot * (counts[:, :128] + before), axis=0, keepdims=True).astype(I32)
        before = before + counts[:, 128:]
        where_at = owner * 256 + place
        addr[chunk : chunk + 1, :] = where_at
        row = one_hot_rows(where_at >> 7, 2 * n_track)
        lane = one_hot_rows(where_at & 127, 128)
        high = jnp.broadcast_to((cell >> 7) & 63, row.shape).astype(F32)
        low = jnp.broadcast_to(cell & 127, row.shape).astype(F32)
        values = jnp.concatenate([row * high, row * low], axis=0)
        asks = asks + mxu(values.astype(BF16), lane.astype(BF16), NT)
    ask[...] = jnp.zeros(ask.shape, I32)
    cells = (asks[: 2 * n_track] * 128.0 + asks[2 * n_track :]).astype(I32)
    for owner in range(n_track):
        ask[owner, 0:2, :] = cells[2 * owner : 2 * owner + 2, :]

    def send_ask(step, _):
        other = partner(step)
        remote(ask.at[other], asked.at[track], ask_send.at[other], ask_recv.at[track], (head, other)).start()
        return 0

    own_ask = pltpu.make_async_copy(ask.at[track], asked.at[track], ask_send.at[track])
    own_ask.start()
    lax.fori_loop(1, n_track, send_ask, 0)

    loads[1].wait()
    loads[2].wait()
    brick_wait(pot_hbm, 0, 0, pot, halo_send, halo_recv)

    rows_at = 32
    lanes = lax.broadcasted_iota(I32, (rows_at, 128), 1)
    first, last = lanes == 0, lanes == 127

    def plane(source, x, row, carried):
        o = ROW0 + row
        rows = slice(o, o + rows_at)
        return relax_rows(
            None,
            source[x + 1, rows, :],
            source[x + 2, rows, :],
            source[x + 1, o - 1 : o - 1 + rows_at, :],
            source[x + 1, o + 1 : o + 1 + rows_at, :],
            src[x, row : row + rows_at, :],
            carried,
            first,
            last,
        )

    for row in range(0, n_y, rows_at):
        rows = slice(ROW0 + row, ROW0 + row + rows_at)

        def step(x, carried):
            mid[x + 1, rows, :], carried = plane(pot, x, row, carried)
            return carried

        lax.fori_loop(0, n_x, step, face(pot[0, rows, :], pot[1, rows, :]), unroll=8)

    start(brick_halo(mid, 1, ROW0, mid, mid_send, mid_recv))

    def set_lhs(tile, value, comp):
        high = value.astype(BF16).astype(F32)
        lhs[pl.ds(16 * tile + comp, value.shape[0], stride=16), :] = high
        lhs[pl.ds(16 * tile + 8 + comp, value.shape[0], stride=16), :] = value - high

    lhs[...] = jnp.zeros(lhs.shape, F32)
    loads[7].wait()
    loads[8].wait()
    rim_wait(edge.at[0], rim, 0)
    for comp in range(3):
        set_lhs(1, state[comp], comp)
        lhs[comp : comp + 1, :] = rim[0, comp : comp + 1, :].astype(BF16).astype(F32)
        lhs[8 + comp : 9 + comp, :] = rim[0, comp : comp + 1, :] - lhs[comp : comp + 1, :]
        at = 16 * (n_tiles + 1) + comp
        lhs[at : at + 1, :] = rim[1, comp : comp + 1, :].astype(BF16).astype(F32)
        lhs[at + 8 : at + 9, :] = rim[1, comp : comp + 1, :] - lhs[at : at + 1, :]

    def split_tile(k, _):
        self_high[k], self_low[k] = split(tself[k])
        next_high[k], next_low[k] = split(tnext[k])
        return 0

    lax.fori_loop(0, n_tiles, split_tile, 0, unroll=2)

    def get_lhs(tile):
        return lhs[pl.ds(pl.multiple_of(16 * tile, 16), 16), :].astype(BF16)

    def fold(parts):
        return parts[:8] + parts[8:]

    def exchange(k, _):
        own, low, high = get_lhs(k + 1), get_lhs(k), get_lhs(k + 2)
        parts = mxu(own, self_high[k], NT) + mxu(own, self_low[k], NT)
        parts = parts + (mxu(low, next_high[k], NT) + mxu(low, next_low[k], NT))
        parts = parts + (mxu(high, next_high[k], NN) + mxu(high, next_low[k], NN))
        ex[pl.ds(pl.multiple_of(8 * k, 8), 8), :] = fold(parts)
        return 0

    lax.fori_loop(0, n_tiles, exchange, 0, unroll=4)

    def get_ex(comp):
        return ex[pl.ds(comp, n_tiles, stride=8), :]

    first_ex = [get_ex(comp) for comp in range(3)]
    for comp in range(3):
        field[comp] = first_ex[comp]

    loads[4].wait()
    rows8 = lax.broadcasted_iota(I32, (8, 128), 0)
    kernels = []
    for odd in range(2):
        weights = jnp.zeros((8, 128), F32)
        for comp in range(3):
            weights = weights + jnp.where(
                rows8 == 2 * comp + odd, jnp.broadcast_to(dk[comp : comp + 1, :], (8, 128)), 0.0
            )
        high = weights.astype(BF16).astype(F32)
        kernels.append(jnp.concatenate([high, weights - high], axis=0).astype(BF16))

    brick_wait(mid, 1, ROW0, mid, mid_send, mid_recv)

    for row in range(0, n_y, rows_at):
        rows = slice(ROW0 + row, ROW0 + row + rows_at)

        def step2(x, carried):
            pot[x + 1, rows, :], carried = plane(mid, x, row, carried)
            return carried

        lax.fori_loop(0, n_x, step2, face(mid[0, rows, :], mid[1, rows, :]), unroll=8)

    store = pltpu.make_async_copy(pot.at[pl.ds(1, n_x), inner, :], out_hbm, out_sem.at[0])
    store.start()

    def surface(pair, _):
        total = jnp.zeros((8, 128), F32)
        for odd in range(2):
            high, low = split(pot[2 * pair + odd + 1, ROW0 : ROW0 + n_y, :])
            total = total + fold(mxu(kernels[odd], high, NT)) + fold(mxu(kernels[odd], low, NT))
        surf[pl.ds(pl.multiple_of(8 * pair, 8), 8), :] = total
        return 0

    lax.fori_loop(0, n_x // 2, surface, 0, unroll=4)

    own_ask.wait()

    def wait_ask(step, _):
        other = partner(step)
        copy = remote(ask.at[other], asked.at[other], ask_send.at[other], ask_recv.at[other], (head, other))
        copy.wait_send()
        copy.wait_recv()
        return 0

    lax.fori_loop(1, n_track, wait_ask, 0)
    table = halves(surf[...])

    def reply(step, _):
        other = partner(step)
        low, high = lookup(table, [asked[other, 0:1, :], asked[other, 1:2, :]])
        answer[other] = jnp.where(rows8 % 2 == 0, low, pltpu.roll(high, 1, 0))

        @pl.when(step > 0)
        def _():
            remote(answer.at[other], answered.at[track], ans_send.at[other], ans_recv.at[track], (head, other)).start()

        return 0

    lax.fori_loop(0, n_track, reply, 0)
    own_answer = pltpu.make_async_copy(answer.at[track], answered.at[track], ans_send.at[track])
    own_answer.start()
    own_answer.wait()

    loads[5].wait()
    loads[6].wait()
    profile = jnp.broadcast_to(prof[...], (8, 128))
    temp = jnp.concatenate(
        [
            jnp.take_along_axis(profile, tidx[at : at + 8, :], axis=1)
            for at in range(0, n_tiles, 8)
        ],
        axis=0,
    )
    target = 0.05 + jnp.maximum(1.0 - temp, 0.0)

    def wait_answer(step, _):
        other = partner(step)
        copy = remote(answer.at[other], answered.at[other], ans_send.at[other], ans_recv.at[other], (head, other))
        copy.wait_send()
        copy.wait_recv()
        return 0

    lax.fori_loop(1, n_track, wait_answer, 0)
    table = halves(answered[...].reshape(8 * n_track, 128))

    applied = [[] for _ in range(3)]
    for pair in range(n_tiles // 2):
        found = lookup(table, [addr[2 * pair + i : 2 * pair + i + 1, :] for i in range(2)])
        for value in found:
            for comp in range(3):
                applied[comp].append(value[2 * comp : 2 * comp + 1, :])
    applied = [jnp.concatenate(rows, axis=0) for rows in applied]

    state = llb_section(state, [a + field[comp] for comp, a in enumerate(applied)], target)
    put_edges(1, state)
    start(rim_copies(edge.at[1], rim_new, 2))

    lhs[0:16, :] = jnp.zeros((16, 128), F32)
    lhs[16 * (n_tiles + 1) :, :] = jnp.zeros((16, 128), F32)
    for comp in range(3):
        set_lhs(1, state[comp], comp)
    lax.fori_loop(0, n_tiles, exchange, 0, unroll=4)
    rim_wait(edge.at[1], rim_new, 2)
    end = n_tiles - 1
    for side, tile, dims in ((0, 0, NT), (1, end, NN)):
        high = rim_new[side].astype(BF16).astype(F32)
        both = jnp.concatenate([high, rim_new[side] - high], axis=0).astype(BF16)
        parts = mxu(both, next_high[tile], dims) + mxu(both, next_low[tile], dims)
        ex[8 * tile : 8 * tile + 8, :] = ex[8 * tile : 8 * tile + 8, :] + fold(parts)
    state = llb_section(state, [a + get_ex(comp) for comp, a in enumerate(applied)], target)
    for comp in range(3):
        mag[comp] = state[comp]
    result = pltpu.make_async_copy(mag, mout_hbm, out_sem.at[1])
    result.start()
    result.wait()
    store.wait()


def per_device(n_head, n_track, potential, source, depth_kernel, magnet, footprint, temp_index, temp_profile, self_tiles, next_tiles):
    n_x, n_y, n_z = potential.shape
    n_tiles, width = self_tiles.shape[1], self_tiles.shape[2]
    any_space = pl.BlockSpec(memory_space=pl.ANY)
    dma = pltpu.SemaphoreType.DMA
    relaxed, magnet_out = pl.pallas_call(
        functools.partial(kernel, n_head, n_track),
        out_shape=(
            jax.ShapeDtypeStruct(potential.shape, F32),
            jax.ShapeDtypeStruct((3, n_tiles, width), F32),
        ),
        in_specs=[any_space] * 9,
        out_specs=(any_space, any_space),
        scratch_shapes=[
            pltpu.VMEM((n_x + 2, n_y + 16, n_z), F32),
            pltpu.VMEM((n_x + 2, n_y + 16, n_z), F32),
            pltpu.VMEM((n_x, n_y, n_z), F32),
            pltpu.VMEM((3, n_z), F32),
            pltpu.VMEM((3, n_tiles, width), F32),
            pltpu.VMEM((n_tiles, width), I32),
            pltpu.VMEM((n_tiles, width), I32),
            pltpu.VMEM((1, 128), F32),
            pltpu.VMEM((n_tiles, width, width), F32),
            pltpu.VMEM((n_tiles, width, width), F32),
            pltpu.VMEM((n_tiles, width, width), BF16),
            pltpu.VMEM((n_tiles, width, width), BF16),
            pltpu.VMEM((n_tiles, width, width), BF16),
            pltpu.VMEM((n_tiles, width, width), BF16),
            pltpu.VMEM((16 * (n_tiles + 2), width), F32),
            pltpu.VMEM((8 * n_tiles, width), F32),
            pltpu.VMEM((2, 8, width), F32),
            pltpu.VMEM((2, 8, width), F32),
            pltpu.VMEM((2, 2, 8, width), F32),
            pltpu.VMEM((n_tiles, width), I32),
            pltpu.VMEM((n_track, 8, 128), I32),
            pltpu.VMEM((n_track, 8, 128), I32),
            pltpu.VMEM((8 * (n_x // 2), 128), F32),
            pltpu.VMEM((n_track, 8, 128), F32),
            pltpu.VMEM((n_track, 8, 128), F32),
            pltpu.VMEM((3, n_tiles, width), F32),
            dma((9,)),
            dma((2,)),
            dma((4,)),
            dma((4,)),
            dma((4,)),
            dma((4,)),
            dma((4,)),
            dma((4,)),
            dma((n_track,)),
            dma((n_track,)),
            dma((n_track,)),
            dma((n_track,)),
        ],
        compiler_params=pltpu.CompilerParams(
            collective_id=0, has_side_effects=True, vmem_limit_bytes=48 << 20
        ),
        name="pole_and_grains",
    )(
        potential,
        source,
        depth_kernel,
        magnet.reshape(3, n_tiles, width),
        footprint.reshape(n_tiles, width),
        temp_index.reshape(n_tiles, width),
        temp_profile.reshape(1, -1),
        self_tiles[0],
        next_tiles[0],
    )
    return relaxed, magnet_out.reshape(magnet.shape)


def solution(mesh):
    in_specs = (
        P("head", "track", None),
        P("head", "track", None),
        P(),
        P(None, "track", "head"),
        P("track", "head"),
        P("track", "head"),
        P(),
        P("track", "head", None, None),
        P("track", "head", None, None),
    )
    out_specs = (P("head", "track", None), P(None, "track", "head"))
    return jax.shard_map(
        functools.partial(per_device, mesh.shape["head"], mesh.shape["track"]),
        mesh=mesh,
        in_specs=in_specs,
        out_specs=out_specs,
        check_vma=False,
    )
```

```python
import functools

import jax
import jax.numpy as jnp
from jax import lax
from jax.experimental import pallas as pl
from jax.experimental.pallas import tpu as pltpu
from jax.sharding import PartitionSpec as P

F32 = jnp.float32
BF16 = jnp.bfloat16
I32 = jnp.int32
NN = (((1,), (0,)), ((), ()))
NT = (((1,), (1,)), ((), ()))
ROW0 = 8


def mxu(a, b, dims):
    return lax.dot_general(a, b, dims, preferred_element_type=F32)


def split(a):
    high = a.astype(BF16)
    return high, (a - high.astype(F32)).astype(BF16)


def face(a, b):
    differ = b - a
    perm = 1.0 + pltpu.reciprocal(0.25 + differ * differ)
    return perm, perm * differ


def relax_rows(center, upper, before, after, drive, carried, first, last):
    perm, flux = face(center, upper)
    numer = (drive - carried[1]) + flux
    denom = (1.0 + carried[0]) + perm
    carried = (perm, flux)
    perm, flux = face(before, center)
    numer = numer - flux
    denom = denom + perm
    depth = center.shape[1]
    for other in (
        after,
        jnp.where(last, 0.0, pltpu.roll(center, depth - 1, 1)),
        jnp.where(first, 0.0, pltpu.roll(center, 1, 1)),
    ):
        perm, flux = face(center, other)
        numer = numer + flux
        denom = denom + perm
    return center + (0.8 * numer) * pltpu.reciprocal(denom), carried


def one_hot_rows(index, count):
    lanes = index.shape[1]
    rows = lax.broadcasted_iota(I32, (count, lanes), 0)
    return jnp.where(rows == jnp.broadcast_to(index, (count, lanes)), 1.0, 0.0)


def lookup(table, address):
    hot = jnp.concatenate([one_hot_rows(a & 127, 128) for a in address], axis=1).astype(BF16)
    found = mxu(table, jnp.concatenate([hot, hot], axis=0), NN)
    results = []
    for part, a in enumerate(address):
        group = jnp.broadcast_to(a >> 8, (8, 128))
        odd = jnp.broadcast_to((a >> 7) & 1, (8, 128))
        total = jnp.zeros((8, 128), F32)
        for g in range(table.shape[0] // 8):
            total = total + jnp.where(
                group == g, found[8 * g : 8 * g + 8, 128 * part : 128 * part + 128], 0.0
            )
        results.append(jnp.where(odd == 0, total, pltpu.roll(total, 7, 0)))
    return results


def halves(rows):
    high, low = split(rows)
    return jnp.concatenate([high, low], axis=1)


def llb_section(state, field, target):
    mx, my, mz = state
    sq_norm = mx * mx + my * my + mz * mz
    pull = 0.5 * (1.0 - sq_norm / target)
    hx, hy, hz = (f + pull * m for f, m in zip(field, state))
    tx, ty, tz = my * hz - mz * hy, mz * hx - mx * hz, mx * hy - my * hx
    dx, dy, dz = my * tz - mz * ty, mz * tx - mx * tz, mx * ty - my * tx
    along = 0.3 * (mx * hx + my * hy + mz * hz)
    return tuple(
        m + 0.1 * (along * m - t - 0.5 * d)
        for m, t, d in zip(state, (tx, ty, tz), (dx, dy, dz))
    )


def has_neighbours(n_head, n_track):
    head = lax.axis_index("head")
    track = lax.axis_index("track")
    return head, track, head > 0, head < n_head - 1, track > 0, track < n_track - 1


def remote(a, b, send, recv, device):
    return pltpu.make_async_remote_copy(
        src_ref=a, dst_ref=b, send_sem=send, recv_sem=recv, device_id=device,
        device_id_type=pl.DeviceIdType.MESH,
    )


def start(copies):
    for there, copy in copies:

        @pl.when(there)
        def _():
            copy.start()


def finish(copies):
    for there, copy in copies:

        @pl.when(there)
        def _():
            copy.wait_send()
            copy.wait_recv()


def greet(n_head, n_track):
    head, track, has_low_x, has_high_x, _, _ = has_neighbours(n_head, n_track)
    barrier = pltpu.get_barrier_semaphore()

    def hello(step, _):
        other = (head, lax.rem(track + step, n_track))
        pl.semaphore_signal(barrier, inc=1, device_id=other, device_id_type=pl.DeviceIdType.MESH)
        return 0

    lax.fori_loop(1, n_track, hello, 0)
    for there, other in ((has_low_x, head - 1), (has_high_x, head + 1)):

        @pl.when(there)
        def _():
            pl.semaphore_signal(
                barrier, inc=1, device_id=(other, track), device_id_type=pl.DeviceIdType.MESH
            )

    return barrier, n_track - 1 + has_low_x.astype(I32) + has_high_x.astype(I32)


def rim_copies(n_head, n_track, source, target, send, recv, waits):
    head, track, has_low_x, has_high_x, _, _ = has_neighbours(n_head, n_track)
    low, high = (head - 1, track), (head + 1, track)
    if waits:
        return [
            (has_low_x, remote(source.at[0], target.at[0], send.at[0], recv.at[0], low)),
            (has_high_x, remote(source.at[1], target.at[1], send.at[1], recv.at[1], high)),
        ]
    return [
        (has_low_x, remote(source.at[0], target.at[1], send.at[0], recv.at[1], low)),
        (has_high_x, remote(source.at[1], target.at[0], send.at[1], recv.at[0], high)),
    ]


def put_edges(edge, state):
    edge[...] = jnp.zeros(edge.shape, F32)
    for comp, value in enumerate(state):
        last = value.shape[0] - 1
        edge[0, comp : comp + 1, :] = value[0:1, :]
        edge[1, comp : comp + 1, :] = value[last : last + 1, :]


def rank_grains(foot, addr, ask, n_track):
    later = lax.broadcasted_iota(I32, (128, 128), 0) < lax.broadcasted_iota(I32, (128, 128), 1)
    count_matrix = jnp.concatenate(
        [jnp.where(later, 1.0, 0.0), jnp.ones((128, 128), F32)], axis=1
    ).astype(BF16)
    before = jnp.zeros((n_track, 128), F32)
    asks = jnp.zeros((128, 128), F32)
    for chunk in range(foot.shape[0]):
        cell = foot[chunk : chunk + 1, :]
        owner = cell >> 13
        hot = one_hot_rows(owner, n_track)
        counts = mxu(hot.astype(BF16), count_matrix, NN)
        place = jnp.sum(hot * (counts[:, :128] + before), axis=0, keepdims=True).astype(I32)
        before = before + counts[:, 128:]
        where_at = owner * 256 + place
        addr[chunk : chunk + 1, :] = where_at
        row = one_hot_rows(where_at >> 7, 2 * n_track)
        lane = one_hot_rows(where_at & 127, 128)
        high = jnp.broadcast_to((cell >> 7) & 63, row.shape).astype(F32)
        low = jnp.broadcast_to(cell & 127, row.shape).astype(F32)
        values = jnp.concatenate([row * high, row * low], axis=0)
        asks = asks + mxu(values.astype(BF16), lane.astype(BF16), NT)
    ask[...] = jnp.zeros(ask.shape, I32)
    cells = (asks[: 2 * n_track] * 128.0 + asks[2 * n_track :]).astype(I32)
    for owner in range(n_track):
        ask[owner, 0:2, :] = cells[2 * owner : 2 * owner + 2, :]


def swept(source, src, x, row, rows_at, carried):
    lanes = lax.broadcasted_iota(I32, (rows_at, 128), 1)
    o = ROW0 + row
    rows = slice(o, o + rows_at)
    return relax_rows(
        source[x + 1, rows, :],
        source[x + 2, rows, :],
        source[x + 1, o - 1 : o - 1 + rows_at, :],
        source[x + 1, o + 1 : o + 1 + rows_at, :],
        src[x, row : row + rows_at, :],
        carried,
        lanes == 0,
        lanes == 127,
    )


def first_kernel(
    n_head, n_track,
    pot_hbm, src_hbm, mag_hbm, foot_hbm,
    mid, src, asked, addr, rim,
    pot, mag, foot, ask, edge,
    in_sem, halo_send, halo_recv, mid_send, mid_recv, rim_send, rim_recv, ask_send, ask_recv,
):
    head, track, has_low_x, has_high_x, has_low_y, has_high_y = has_neighbours(n_head, n_track)
    n_x, n_y, n_z = src.shape
    inner, all_x = pl.ds(ROW0, n_y), pl.ds(1, n_x)
    low_x, high_x = (head - 1, track), (head + 1, track)
    low_y, high_y = (head, track - 1), (head, track + 1)

    pairs = [
        (foot_hbm, foot),
        (mag_hbm, mag),
        (pot_hbm, pot.at[all_x, inner, :]),
        (src_hbm, src),
    ]
    loads = [pltpu.make_async_copy(a, b, in_sem.at[i]) for i, (a, b) in enumerate(pairs)]
    for copy in loads:
        copy.start()

    for ref in (pot, mid):
        for plane in (0, n_x + 1):
            ref[plane, ROW0 : ROW0 + n_y, :] = jnp.zeros((n_y, n_z), F32)
        for row in (ROW0 - 1, ROW0 + n_y):
            ref[1 : n_x + 1, row : row + 1, :] = jnp.zeros((n_x, 1, n_z), F32)
    rim[...] = jnp.zeros(rim.shape, F32)
    barrier, n_greeted = greet(n_head, n_track)
    loads[1].wait()
    put_edges(edge, [mag[comp] for comp in range(3)])
    pl.semaphore_wait(barrier, n_greeted)

    def halo(source, plane, row, target, send, recv):
        rows, planes = pl.ds(row, n_y), pl.ds(plane, n_x)
        return [
            (has_low_x, remote(source.at[plane, rows, :], target.at[n_x + 1, inner, :], send.at[0], recv.at[1], low_x)),
            (has_high_x, remote(source.at[plane + n_x - 1, rows, :], target.at[0, inner, :], send.at[1], recv.at[0], high_x)),
            (has_low_y, remote(source.at[planes, pl.ds(row, 1), :], target.at[all_x, pl.ds(ROW0 + n_y, 1), :], send.at[2], recv.at[3], low_y)),
            (has_high_y, remote(source.at[planes, pl.ds(row + n_y - 1, 1), :], target.at[all_x, pl.ds(ROW0 - 1, 1), :], send.at[3], recv.at[2], high_y)),
        ]

    def halo_waits(source, plane, row, target, send, recv):
        rows, planes = pl.ds(row, n_y), pl.ds(plane, n_x)
        return [
            (has_low_x, remote(source.at[plane, rows, :], target.at[0, inner, :], send.at[0], recv.at[0], low_x)),
            (has_high_x, remote(source.at[plane + n_x - 1, rows, :], target.at[n_x + 1, inner, :], send.at[1], recv.at[1], high_x)),
            (has_low_y, remote(source.at[planes, pl.ds(row, 1), :], target.at[all_x, pl.ds(ROW0 - 1, 1), :], send.at[2], recv.at[2], low_y)),
            (has_high_y, remote(source.at[planes, pl.ds(row + n_y - 1, 1), :], target.at[all_x, pl.ds(ROW0 + n_y, 1), :], send.at[3], recv.at[3], high_y)),
        ]

    start(halo(pot_hbm, 0, 0, pot, halo_send, halo_recv))
    start(rim_copies(n_head, n_track, edge, rim, rim_send, rim_recv, False))

    loads[0].wait()
    rank_grains(foot, addr, ask, n_track)
    asked[track] = ask[track]

    def send_ask(step, _):
        other = lax.rem(track + step, n_track)
        remote(ask.at[other], asked.at[track], ask_send.at[other], ask_recv.at[track], (head, other)).start()
        return 0

    lax.fori_loop(1, n_track, send_ask, 0)

    loads[2].wait()
    loads[3].wait()
    finish(halo_waits(pot_hbm, 0, 0, pot, halo_send, halo_recv))
    rows_at = 32
    chunks = range(0, n_y, rows_at)
    for x in (0, n_x - 1):
        for row in chunks:
            rows = slice(ROW0 + row, ROW0 + row + rows_at)
            mid[x + 1, rows, :], _ = swept(pot, src, x, row, rows_at, face(pot[x, rows, :], pot[x + 1, rows, :]))
    outer = halo(mid, 1, ROW0, mid, mid_send, mid_recv)
    start(outer[:2])
    unroll = 8
    for row in [chunks[0], chunks[-1], *chunks[1:-1]]:
        rows = slice(ROW0 + row, ROW0 + row + rows_at)

        def planes(base, count, carried):
            for j in range(count):
                mid[base + j + 1, rows, :], carried = swept(pot, src, base + j, row, rows_at, carried)
            return carried

        carried = face(pot[1, rows, :], pot[2, rows, :])
        trips = (n_x - 2) // unroll
        carried = lax.fori_loop(0, trips, lambda i, c: planes(1 + unroll * i, unroll, c), carried)
        planes(1 + unroll * trips, n_x - 2 - unroll * trips, carried)
        if row == chunks[-1]:
            start(outer[2:])

    def wait_ask(step, _):
        other = lax.rem(track + step, n_track)
        copy = remote(ask.at[other], asked.at[other], ask_send.at[other], ask_recv.at[other], (head, other))
        copy.wait_send()
        copy.wait_recv()
        return 0

    lax.fori_loop(1, n_track, wait_ask, 0)
    finish(rim_copies(n_head, n_track, edge, rim, rim_send, rim_recv, True))
    finish(halo_waits(mid, 1, ROW0, mid, mid_send, mid_recv))


def second_kernel(mid, src, asked, dk_hbm, out_hbm, answer, relaxed, dk, surf, carry, in_sem, out_sem):
    n_x, n_y, n_z = src.shape
    load = pltpu.make_async_copy(dk_hbm, dk, in_sem)
    load.start()
    load.wait()
    rows8 = lax.broadcasted_iota(I32, (8, 128), 0)
    kernels = []
    for odd in range(2):
        weights = jnp.zeros((8, 128), F32)
        for comp in range(3):
            weights = weights + jnp.where(
                rows8 == 2 * comp + odd, jnp.broadcast_to(dk[comp : comp + 1, :], (8, 128)), 0.0
            )
        high = weights.astype(BF16).astype(F32)
        kernels.append(jnp.concatenate([high, weights - high], axis=0))
    kernels = jnp.concatenate(kernels, axis=0).astype(BF16)
    kernels = jnp.concatenate([kernels, kernels], axis=1)

    rows_at = 32
    for row in range(0, n_y, rows_at):
        carry[0, row : row + rows_at, :], carry[1, row : row + rows_at, :] = face(
            mid[0, ROW0 + row : ROW0 + row + rows_at, :], mid[1, ROW0 + row : ROW0 + row + rows_at, :]
        )

    def pair(i, _):
        both = []
        for row in range(0, n_y, rows_at):
            here = slice(row, row + rows_at)
            carried = carry[0, here, :], carry[1, here, :]
            for odd in range(2):
                value, carried = swept(mid, src, 2 * i + odd, row, rows_at, carried)
                relaxed[2 * i + odd, here, :] = value
            carry[0, here, :], carry[1, here, :] = carried
        for odd in range(2):
            both.append(halves(relaxed[2 * i + odd]))
        pltpu.make_async_copy(relaxed.at[pl.ds(2 * i, 2)], out_hbm.at[pl.ds(2 * i, 2)], out_sem).start()
        found = mxu(kernels, jnp.concatenate(both, axis=0), NT)
        total = (found[0:8, :n_y] + found[8:16, :n_y]) + (found[16:24, n_y:] + found[24:32, n_y:])
        surf[pl.ds(pl.multiple_of(8 * i, 8), 8), :] = total
        return 0

    lax.fori_loop(0, n_x // 2, pair, 0)
    table = halves(surf[...])

    def reply(other, _):
        low, high = lookup(table, [asked[other, 0:1, :], asked[other, 1:2, :]])
        answer[other] = jnp.where(rows8 % 2 == 0, low, pltpu.roll(high, 1, 0))
        return 0

    lax.fori_loop(0, answer.shape[0], reply, 0, unroll=4)
    pltpu.make_async_copy(relaxed, out_hbm, out_sem).wait()


def third_kernel(
    n_head, n_track,
    answer, addr, rim, mag_hbm, temp_hbm, prof_hbm, self_hbm, next_hbm,
    mout_hbm,
    answered, mag, tidx, prof, tself, tnext, near_high, near_low, above, lhs, ex, rim_new, edge,
    in_sem, out_sem, rim_send, rim_recv, ans_send, ans_recv,
):
    head, track, *_ = has_neighbours(n_head, n_track)
    n_tiles, width = mag.shape[1:]
    pairs = [(self_hbm, tself), (next_hbm, tnext), (mag_hbm, mag), (temp_hbm, tidx), (prof_hbm, prof)]
    loads = [pltpu.make_async_copy(a, b, in_sem.at[i]) for i, (a, b) in enumerate(pairs)]
    for copy in loads:
        copy.start()
    rim_new[...] = jnp.zeros(rim_new.shape, F32)
    barrier, n_greeted = greet(n_head, n_track)

    def set_lhs(tile, value, comp):
        high = value.astype(BF16).astype(F32)
        lhs[pl.ds(16 * tile + comp, value.shape[0], stride=16), :] = high
        lhs[pl.ds(16 * tile + 8 + comp, value.shape[0], stride=16), :] = value - high

    lhs[...] = jnp.zeros(lhs.shape, F32)
    for copy in loads:
        copy.wait()
    for side, tile in ((0, 0), (1, n_tiles + 1)):
        high = rim[side].astype(BF16).astype(F32)
        lhs[16 * tile : 16 * tile + 8, :] = high
        lhs[16 * tile + 8 : 16 * tile + 16, :] = rim[side] - high
    state = [mag[comp] for comp in range(3)]
    for comp in range(3):
        set_lhs(1, state[comp], comp)
    profile = jnp.broadcast_to(prof[...], (8, 128))
    temp = jnp.concatenate(
        [jnp.take_along_axis(profile, tidx[at : at + 8, :], axis=1) for at in range(0, n_tiles, 8)], axis=0
    )
    target = 0.05 + jnp.maximum(1.0 - temp, 0.0)

    pl.semaphore_wait(barrier, n_greeted)
    answered[track] = answer[track]

    def send_answer(step, _):
        other = lax.rem(track + step, n_track)
        remote(answer.at[other], answered.at[track], ans_send.at[other], ans_recv.at[track], (head, other)).start()
        return 0

    lax.fori_loop(1, n_track, send_answer, 0)

    def get_lhs(tile):
        return lhs[pl.ds(pl.multiple_of(16 * tile, 16), 16), :].astype(BF16)

    def fold(parts):
        return parts[:8] + parts[8:]

    def exchange(k):
        near = jnp.concatenate([get_lhs(k + 1), get_lhs(k)], axis=1)
        far = get_lhs(k + 2)
        parts = mxu(near, near_high[k], NT) + mxu(near, near_low[k], NT)
        parts = parts + mxu(jnp.concatenate([far, far], axis=1), above[k], NN)
        ex[pl.ds(pl.multiple_of(8 * k, 8), 8), :] = fold(parts)

    def first_exchange(k, _):
        self_high, self_low = split(tself[k])
        next_high, next_low = split(tnext[k])
        near_high[k] = jnp.concatenate([self_high, next_high], axis=1)
        near_low[k] = jnp.concatenate([self_low, next_low], axis=1)
        above[k] = jnp.concatenate([next_high, next_low], axis=0)
        exchange(k)
        return 0

    def next_exchange(k, _):
        exchange(k)
        return 0

    def get_ex(comp):
        return ex[pl.ds(comp, n_tiles, stride=8), :]

    lax.fori_loop(0, n_tiles, first_exchange, 0, unroll=4)

    def wait_answer(step, _):
        other = lax.rem(track + step, n_track)
        copy = remote(answer.at[other], answered.at[other], ans_send.at[other], ans_recv.at[other], (head, other))
        copy.wait_send()
        copy.wait_recv()
        return 0

    lax.fori_loop(1, n_track, wait_answer, 0)
    table = halves(answered[...].reshape(8 * n_track, 128))
    applied = [[] for _ in range(3)]
    for pair in range(n_tiles // 2):
        found = lookup(table, [addr[2 * pair + i : 2 * pair + i + 1, :] for i in range(2)])
        for value in found:
            for comp in range(3):
                applied[comp].append(value[2 * comp : 2 * comp + 1, :])
    applied = [jnp.concatenate(rows, axis=0) for rows in applied]

    state = llb_section(state, [a + get_ex(comp) for comp, a in enumerate(applied)], target)
    put_edges(edge, state)
    start(rim_copies(n_head, n_track, edge, rim_new, rim_send, rim_recv, False))

    lhs[0:16, :] = jnp.zeros((16, width), F32)
    lhs[16 * (n_tiles + 1) :, :] = jnp.zeros((16, width), F32)
    for comp in range(3):
        set_lhs(1, state[comp], comp)
    lax.fori_loop(0, n_tiles, next_exchange, 0, unroll=4)
    finish(rim_copies(n_head, n_track, edge, rim_new, rim_send, rim_recv, True))
    end = n_tiles - 1
    for side, tile in ((0, 0), (1, end)):
        high = rim_new[side].astype(BF16).astype(F32)
        both = jnp.concatenate([high, rim_new[side] - high], axis=0).astype(BF16)
        if side == 0:
            parts = mxu(both, near_high[tile][:, width:], NT) + mxu(both, near_low[tile][:, width:], NT)
        else:
            parts = mxu(jnp.concatenate([both, both], axis=1), above[tile], NN)
        ex[8 * tile : 8 * tile + 8, :] = ex[8 * tile : 8 * tile + 8, :] + fold(parts)
    state = llb_section(state, [a + get_ex(comp) for comp, a in enumerate(applied)], target)
    for comp in range(3):
        mag[comp] = state[comp]
    result = pltpu.make_async_copy(mag, mout_hbm, out_sem)
    result.start()
    result.wait()


def per_device(n_head, n_track, potential, source, depth_kernel, magnet, footprint, temp_index, temp_profile, self_tiles, next_tiles):
    n_x, n_y, n_z = potential.shape
    n_tiles, width = self_tiles.shape[1], self_tiles.shape[2]
    padded = (n_x + 2, n_y + 16, n_z)
    hbm, vmem, dma = pltpu.HBM, pltpu.VMEM, pltpu.SemaphoreType.DMA
    in_hbm = pl.BlockSpec(memory_space=hbm)
    in_vmem = pl.BlockSpec(memory_space=vmem)

    def stay(*arrays):
        return [pltpu.with_memory_space_constraint(a, hbm) for a in arrays]

    potential, source, depth_kernel, magnet_in, footprint, temp_index, temp_profile, self_tiles, next_tiles = stay(
        potential,
        source,
        depth_kernel,
        magnet.reshape(3, n_tiles, width),
        footprint.reshape(n_tiles, width),
        temp_index.reshape(n_tiles, width),
        temp_profile.reshape(1, -1),
        self_tiles[0],
        next_tiles[0],
    )
    listed = (n_track, 8, width)
    mid, src, asked, addr, rim = pl.pallas_call(
        functools.partial(first_kernel, n_head, n_track),
        out_shape=(
            vmem(padded, F32),
            vmem((n_x, n_y, n_z), F32),
            vmem(listed, I32),
            vmem((n_tiles, width), I32),
            vmem((2, 8, width), F32),
        ),
        in_specs=[in_hbm] * 4,
        out_specs=(in_vmem,) * 5,
        scratch_shapes=[
            vmem(padded, F32),
            vmem((3, n_tiles, width), F32),
            vmem((n_tiles, width), I32),
            vmem(listed, I32),
            vmem((2, 8, width), F32),
            dma((4,)),
            *[dma((4,))] * 4,
            *[dma((2,))] * 2,
            *[dma((n_track,))] * 2,
        ],
        compiler_params=pltpu.CompilerParams(
            collective_id=0, has_side_effects=True, vmem_limit_bytes=10 << 20
        ),
        name="first_sweep",
    )(potential, source, magnet_in, footprint)
    relaxed, answer = pl.pallas_call(
        second_kernel,
        out_shape=(hbm((n_x, n_y, n_z), F32), vmem(listed, F32)),
        in_specs=[in_vmem] * 3 + [in_hbm],
        out_specs=(in_hbm, in_vmem),
        scratch_shapes=[
            vmem((n_x, n_y, n_z), F32),
            vmem((3, n_z), F32),
            vmem((8 * (n_x // 2), n_y), F32),
            vmem((2, n_y, n_z), F32),
            dma,
            dma,
        ],
        compiler_params=pltpu.CompilerParams(vmem_limit_bytes=10 << 20),
        name="second_sweep",
    )(mid, src, asked, depth_kernel)
    magnet_out = pl.pallas_call(
        functools.partial(third_kernel, n_head, n_track),
        out_shape=hbm((3, n_tiles, width), F32),
        in_specs=[in_vmem] * 3 + [in_hbm] * 5,
        out_specs=in_hbm,
        scratch_shapes=[
            vmem(listed, F32),
            vmem((3, n_tiles, width), F32),
            vmem((n_tiles, width), I32),
            vmem((1, 128), F32),
            vmem((n_tiles, width, width), F32),
            vmem((n_tiles, width, width), F32),
            vmem((n_tiles, width, 2 * width), BF16),
            vmem((n_tiles, width, 2 * width), BF16),
            vmem((n_tiles, 2 * width, width), BF16),
            vmem((16 * (n_tiles + 2), width), F32),
            vmem((8 * n_tiles, width), F32),
            vmem((2, 8, width), F32),
            vmem((2, 8, width), F32),
            dma((5,)),
            dma,
            *[dma((2,))] * 2,
            *[dma((n_track,))] * 2,
        ],
        compiler_params=pltpu.CompilerParams(
            collective_id=1, has_side_effects=True, vmem_limit_bytes=16 << 20
        ),
        name="sections",
    )(answer, addr, rim, magnet_in, temp_index, temp_profile, self_tiles, next_tiles)
    return relaxed, magnet_out.reshape(magnet.shape)


def solution(mesh):
    in_specs = (
        P("head", "track", None),
        P("head", "track", None),
        P(),
        P(None, "track", "head"),
        P("track", "head"),
        P("track", "head"),
        P(),
        P("track", "head", None, None),
        P("track", "head", None, None),
    )
    out_specs = (P("head", "track", None), P(None, "track", "head"))
    return jax.shard_map(
        functools.partial(per_device, mesh.shape["head"], mesh.shape["track"]),
        mesh=mesh,
        in_specs=in_specs,
        out_specs=out_specs,
        check_vma=False,
    )
```

```python
import functools

import jax
import jax.numpy as jnp
from jax import lax
from jax.experimental import pallas as pl
from jax.experimental.pallas import tpu as pltpu
from jax.sharding import PartitionSpec as P

F32 = jnp.float32
BF16 = jnp.bfloat16
I32 = jnp.int32
NN = (((1,), (0,)), ((), ()))
NT = (((1,), (1,)), ((), ()))
ROW0 = 8
EARLY = 16


def mxu(a, b, dims):
    return lax.dot_general(a, b, dims, preferred_element_type=F32)


def split(a):
    high = a.astype(BF16)
    return high, (a - high.astype(F32)).astype(BF16)


def face(a, b):
    differ = b - a
    perm = 1.0 + pltpu.reciprocal(0.25 + differ * differ)
    return perm, perm * differ


def relax_rows(center, upper, before, after, drive, carried, first, last):
    perm, flux = face(center, upper)
    numer = (drive - carried[1]) + flux
    denom = (1.0 + carried[0]) + perm
    carried = (perm, flux)
    perm, flux = face(before, center)
    numer = numer - flux
    denom = denom + perm
    depth = center.shape[1]
    for other in (
        after,
        jnp.where(last, 0.0, pltpu.roll(center, depth - 1, 1)),
        jnp.where(first, 0.0, pltpu.roll(center, 1, 1)),
    ):
        perm, flux = face(center, other)
        numer = numer + flux
        denom = denom + perm
    return center + (0.8 * numer) * pltpu.reciprocal(denom), carried


def one_hot_rows(index, count):
    lanes = index.shape[1]
    rows = lax.broadcasted_iota(I32, (count, lanes), 0)
    return jnp.where(rows == jnp.broadcast_to(index, (count, lanes)), 1.0, 0.0)


def lookup(table, address):
    hot = jnp.concatenate([one_hot_rows(a & 127, 128) for a in address], axis=1).astype(BF16)
    found = mxu(table, jnp.concatenate([hot, hot], axis=0), NN)
    results = []
    for part, a in enumerate(address):
        group = jnp.broadcast_to(a >> 8, (8, 128))
        odd = jnp.broadcast_to((a >> 7) & 1, (8, 128))
        total = jnp.zeros((8, 128), F32)
        for g in range(table.shape[0] // 8):
            total = total + jnp.where(
                group == g, found[8 * g : 8 * g + 8, 128 * part : 128 * part + 128], 0.0
            )
        results.append(jnp.where(odd == 0, total, pltpu.roll(total, 7, 0)))
    return results


def halves(rows):
    high, low = split(rows)
    return jnp.concatenate([high, low], axis=1)


def llb_section(state, field, target):
    mx, my, mz = state
    sq_norm = mx * mx + my * my + mz * mz
    pull = 0.5 * (1.0 - sq_norm / target)
    hx, hy, hz = (f + pull * m for f, m in zip(field, state))
    tx, ty, tz = my * hz - mz * hy, mz * hx - mx * hz, mx * hy - my * hx
    dx, dy, dz = my * tz - mz * ty, mz * tx - mx * tz, mx * ty - my * tx
    along = 0.3 * (mx * hx + my * hy + mz * hz)
    return tuple(
        m + 0.1 * (along * m - t - 0.5 * d)
        for m, t, d in zip(state, (tx, ty, tz), (dx, dy, dz))
    )


def has_neighbours(n_head, n_track):
    head = lax.axis_index("head")
    track = lax.axis_index("track")
    return head, track, head > 0, head < n_head - 1, track > 0, track < n_track - 1


def remote(a, b, send, recv, device):
    return pltpu.make_async_remote_copy(
        src_ref=a, dst_ref=b, send_sem=send, recv_sem=recv, device_id=device,
        device_id_type=pl.DeviceIdType.MESH,
    )


def start(copies):
    for there, copy in copies:

        @pl.when(there)
        def _():
            copy.start()


def finish(copies):
    for there, copy in copies:

        @pl.when(there)
        def _():
            copy.wait_send()
            copy.wait_recv()


def greet(n_head, n_track):
    head, track, has_low_x, has_high_x, _, _ = has_neighbours(n_head, n_track)
    barrier = pltpu.get_barrier_semaphore()

    def hello(step, _):
        other = (head, lax.rem(track + step, n_track))
        pl.semaphore_signal(barrier, inc=1, device_id=other, device_id_type=pl.DeviceIdType.MESH)
        return 0

    lax.fori_loop(1, n_track, hello, 0)
    for there, other in ((has_low_x, head - 1), (has_high_x, head + 1)):

        @pl.when(there)
        def _():
            pl.semaphore_signal(
                barrier, inc=1, device_id=(other, track), device_id_type=pl.DeviceIdType.MESH
            )

    return barrier, n_track - 1 + has_low_x.astype(I32) + has_high_x.astype(I32)


def rim_copies(n_head, n_track, source, target, send, recv, waits):
    head, track, has_low_x, has_high_x, _, _ = has_neighbours(n_head, n_track)
    low, high = (head - 1, track), (head + 1, track)
    if waits:
        return [
            (has_low_x, remote(source.at[0], target.at[0], send.at[0], recv.at[0], low)),
            (has_high_x, remote(source.at[1], target.at[1], send.at[1], recv.at[1], high)),
        ]
    return [
        (has_low_x, remote(source.at[0], target.at[1], send.at[0], recv.at[1], low)),
        (has_high_x, remote(source.at[1], target.at[0], send.at[1], recv.at[0], high)),
    ]


def put_edges(edge, state):
    edge[...] = jnp.zeros(edge.shape, F32)
    for comp, value in enumerate(state):
        last = value.shape[0] - 1
        edge[0, comp : comp + 1, :] = value[0:1, :]
        edge[1, comp : comp + 1, :] = value[last : last + 1, :]


def rank_grains(foot, addr, ask, n_track):
    later = lax.broadcasted_iota(I32, (128, 128), 0) < lax.broadcasted_iota(I32, (128, 128), 1)
    count_matrix = jnp.concatenate(
        [jnp.where(later, 1.0, 0.0), jnp.ones((128, 128), F32)], axis=1
    ).astype(BF16)
    before = jnp.zeros((n_track, 128), F32)
    asks = jnp.zeros((128, 128), F32)
    for chunk in range(foot.shape[0]):
        cell = foot[chunk : chunk + 1, :]
        owner = cell >> 13
        hot = one_hot_rows(owner, n_track)
        counts = mxu(hot.astype(BF16), count_matrix, NN)
        place = jnp.sum(hot * (counts[:, :128] + before), axis=0, keepdims=True).astype(I32)
        before = before + counts[:, 128:]
        where_at = owner * 256 + place
        addr[chunk : chunk + 1, :] = where_at
        row = one_hot_rows(where_at >> 7, 2 * n_track)
        lane = one_hot_rows(where_at & 127, 128)
        high = jnp.broadcast_to((cell >> 7) & 63, row.shape).astype(F32)
        low = jnp.broadcast_to(cell & 127, row.shape).astype(F32)
        values = jnp.concatenate([row * high, row * low], axis=0)
        asks = asks + mxu(values.astype(BF16), lane.astype(BF16), NT)
    cells = (asks[: 2 * n_track] * 128.0 + asks[2 * n_track :]).astype(I32)
    for owner in range(n_track):
        ask[owner, 0:2, :] = cells[2 * owner : 2 * owner + 2, :]


def swept(source, src, x, row, rows_at, carried):
    lanes = lax.broadcasted_iota(I32, (rows_at, 128), 1)
    o = ROW0 + row
    rows = slice(o, o + rows_at)
    return relax_rows(
        source[x + 1, rows, :],
        source[x + 2, rows, :],
        source[x + 1, o - 1 : o - 1 + rows_at, :],
        source[x + 1, o + 1 : o + 1 + rows_at, :],
        src[x, row : row + rows_at, :],
        carried,
        lanes == 0,
        lanes == 127,
    )


def fold(parts):
    return parts[:8] + parts[8:]


def exchange(k, lhs, near_high, near_low, above, ex):
    def get_lhs(tile):
        return lhs[pl.ds(pl.multiple_of(16 * tile, 16), 16), :].astype(BF16)

    near = jnp.concatenate([get_lhs(k + 1), get_lhs(k)], axis=1)
    far = get_lhs(k + 2)
    parts = mxu(near, near_high[k], NT) + mxu(near, near_low[k], NT)
    parts = parts + mxu(jnp.concatenate([far, far], axis=1), above[k], NN)
    ex[pl.ds(pl.multiple_of(8 * k, 8), 8), :] = fold(parts)


def get_ex(ex):
    return [ex[pl.ds(comp, ex.shape[0] // 8, stride=8), :] for comp in range(3)]


def main_kernel(
    n_head, n_track,
    pot_hbm, src_hbm, dk_hbm, mag_hbm, foot_hbm, temp_hbm, prof_hbm, self_hbm, next_hbm,
    pot, near_high, near_low, above, lhs, ex, rim_new, state_out, applied_out, target_out,
    mid, src, dk, mag, foot, tidx, prof, tself, tnext,
    rim, edge, edge_new, lines, lines_in, lines_mid, lines_mid_in,
    addr, ask, asked, surf, answer, answered,
    in_sem, halo_send, halo_recv, mid_send, mid_recv, rim_send, rim_recv,
    rim_new_send, rim_new_recv, ask_send, ask_recv, ans_send, ans_recv,
):
    head, track, has_low_x, has_high_x, has_low_y, has_high_y = has_neighbours(n_head, n_track)
    n_x, n_y, n_z = src.shape
    n_tiles, width = mag.shape[1:]
    inner, all_x = pl.ds(ROW0, n_y), pl.ds(1, n_x)
    low_x, high_x = (head - 1, track), (head + 1, track)
    low_y, high_y = (head, track - 1), (head, track + 1)
    rows8 = lax.broadcasted_iota(I32, (8, 128), 0)

    pairs = [
        (foot_hbm, foot),
        (mag_hbm, mag),
        (pot_hbm.at[:, pl.ds(0, 1), :], lines.at[0]),
        (pot_hbm.at[:, pl.ds(n_y - 1, 1), :], lines.at[1]),
        (pot_hbm, pot.at[all_x, inner, :]),
        (src_hbm, src),
        (dk_hbm, dk),
        (temp_hbm, tidx),
        (prof_hbm, prof),
        (self_hbm, tself),
        (next_hbm, tnext),
    ]
    loads = [pltpu.make_async_copy(a, b, in_sem.at[i]) for i, (a, b) in enumerate(pairs)]
    for copy in loads:
        copy.start()

    for ref in (pot, mid):
        for plane in (0, n_x + 1):
            ref[plane, ROW0 : ROW0 + n_y, :] = jnp.zeros((n_y, n_z), F32)
    lines_in[...] = jnp.zeros(lines_in.shape, F32)
    lines_mid_in[...] = jnp.zeros(lines_mid_in.shape, F32)
    rim[...] = jnp.zeros(rim.shape, F32)
    rim_new[...] = jnp.zeros(rim_new.shape, F32)
    barrier, n_greeted = greet(n_head, n_track)
    loads[0].wait()
    rank_grains(foot, addr, ask, n_track)
    asked[track] = ask[track]
    loads[1].wait()
    put_edges(edge, [mag[comp] for comp in range(3)])
    loads[2].wait()
    loads[3].wait()
    pl.semaphore_wait(barrier, n_greeted)

    def halo(planes, rows, target, rows_in, send, recv):
        return [
            (has_low_x, remote(planes[0], target.at[n_x + 1, inner, :], send.at[0], recv.at[1], low_x)),
            (has_high_x, remote(planes[1], target.at[0, inner, :], send.at[1], recv.at[0], high_x)),
            (has_low_y, remote(rows.at[0], rows_in.at[1], send.at[2], recv.at[3], low_y)),
            (has_high_y, remote(rows.at[1], rows_in.at[0], send.at[3], recv.at[2], high_y)),
        ]

    def halo_waits(planes, rows, target, rows_in, send, recv):
        return [
            (has_low_x, remote(planes[0], target.at[0, inner, :], send.at[0], recv.at[0], low_x)),
            (has_high_x, remote(planes[1], target.at[n_x + 1, inner, :], send.at[1], recv.at[1], high_x)),
            (has_low_y, remote(rows.at[0], rows_in.at[0], send.at[2], recv.at[2], low_y)),
            (has_high_y, remote(rows.at[1], rows_in.at[1], send.at[3], recv.at[3], high_y)),
        ]

    def place_lines(rows_in, target):
        target[1 : n_x + 1, ROW0 - 1 : ROW0, :] = rows_in[0]
        target[1 : n_x + 1, ROW0 + n_y : ROW0 + n_y + 1, :] = rows_in[1]

    start_halo = [pot_hbm.at[0], pot_hbm.at[n_x - 1]], lines, pot, lines_in, halo_send, halo_recv
    start(halo(*start_halo))

    def send_ask(step, _):
        other = lax.rem(track + step, n_track)
        remote(ask.at[other], asked.at[track], ask_send.at[other], ask_recv.at[track], (head, other)).start()
        return 0

    lax.fori_loop(1, n_track, send_ask, 0)
    start(rim_copies(n_head, n_track, edge, rim, rim_send, rim_recv, False))
    loads[4].wait()
    loads[5].wait()

    rows_at = 32
    chunks = list(range(0, n_y, rows_at))
    unroll = 8

    def chunk_rows(row):
        return slice(ROW0 + row, ROW0 + row + rows_at)

    def sweep_chunk(source, target, row):
        rows = chunk_rows(row)

        def planes(base, count, carried):
            for j in range(count):
                target[base + j + 1, rows, :], carried = swept(source, src, base + j, row, rows_at, carried)
            return carried

        carried = face(source[1, rows, :], source[2, rows, :])
        trips = (n_x - 2) // unroll
        carried = lax.fori_loop(0, trips, lambda i, c: planes(1 + unroll * i, unroll, c), carried)
        planes(1 + unroll * trips, n_x - 2 - unroll * trips, carried)

    def sweep_outer(source, target):
        for x in (0, n_x - 1):
            for row in chunks:
                rows = chunk_rows(row)
                carried = face(source[x, rows, :], source[x + 1, rows, :])
                target[x + 1, rows, :], _ = swept(source, src, x, row, rows_at, carried)

    for row in chunks[1:-1]:
        sweep_chunk(pot, mid, row)
    finish(halo_waits(*start_halo))
    place_lines(lines_in, pot)
    sweep_outer(pot, mid)
    mid_halo = [mid.at[1, inner, :], mid.at[n_x, inner, :]], lines_mid, mid, lines_mid_in, mid_send, mid_recv
    sends = halo(*mid_halo)
    start(sends[:2])
    for row in (chunks[0], chunks[-1]):
        sweep_chunk(pot, mid, row)
    lines_mid[0] = mid[1 : n_x + 1, ROW0 : ROW0 + 1, :]
    lines_mid[1] = mid[1 : n_x + 1, ROW0 + n_y - 1 : ROW0 + n_y, :]
    start(sends[2:])

    for row in chunks[1:-1]:
        sweep_chunk(mid, pot, row)
    finish(halo_waits(*mid_halo))
    place_lines(lines_mid_in, mid)
    sweep_outer(mid, pot)
    for row in (chunks[0], chunks[-1]):
        sweep_chunk(mid, pot, row)

    loads[6].wait()
    kernels = []
    for odd in range(2):
        weights = jnp.zeros((8, 128), F32)
        for comp in range(3):
            weights = weights + jnp.where(
                rows8 == 2 * comp + odd, jnp.broadcast_to(dk[comp : comp + 1, :], (8, 128)), 0.0
            )
        high = weights.astype(BF16).astype(F32)
        kernels.append(jnp.concatenate([high, weights - high], axis=0))
    kernels = jnp.concatenate(kernels, axis=0).astype(BF16)
    kernels = jnp.concatenate([kernels, kernels], axis=1)

    def surface(i, _):
        both = [halves(pot[2 * i + odd + 1, ROW0 : ROW0 + n_y, :]) for odd in range(2)]
        found = mxu(kernels, jnp.concatenate(both, axis=0), NT)
        total = (found[0:8, :n_y] + found[8:16, :n_y]) + (found[16:24, n_y:] + found[24:32, n_y:])
        surf[pl.ds(pl.multiple_of(8 * i, 8), 8), :] = total
        return 0

    lax.fori_loop(0, n_x // 2, surface, 0, unroll=8)

    def wait_ask(step, _):
        other = lax.rem(track + step, n_track)
        copy = remote(ask.at[other], asked.at[other], ask_send.at[other], ask_recv.at[other], (head, other))
        copy.wait_send()
        copy.wait_recv()
        return 0

    lax.fori_loop(1, n_track, wait_ask, 0)
    table = halves(surf[...])

    def reply(group, own):
        for j in range(4):
            step = 4 * group + j
            other = lax.rem(track + step, n_track)
            low, high = lookup(table, [asked[other, 0:1, :], asked[other, 1:2, :]])
            tile = jnp.where(rows8 % 2 == 0, low, pltpu.roll(high, 1, 0))
            if own and j == 0:
                answered[track] = tile
            else:
                answer[other] = tile
                remote(answer.at[other], answered.at[track], ans_send.at[other], ans_recv.at[track], (head, other)).start()
        return 0

    reply(0, True)
    lax.fori_loop(1, n_track // 4, lambda group, _: reply(group, False), 0)

    def set_lhs(tile, value, comp):
        high = value.astype(BF16).astype(F32)
        lhs[pl.ds(16 * tile + comp, value.shape[0], stride=16), :] = high
        lhs[pl.ds(16 * tile + 8 + comp, value.shape[0], stride=16), :] = value - high

    lhs[...] = jnp.zeros(lhs.shape, F32)
    finish(rim_copies(n_head, n_track, edge, rim, rim_send, rim_recv, True))
    for side, tile in ((0, 0), (1, n_tiles + 1)):
        high = rim[side].astype(BF16).astype(F32)
        lhs[16 * tile : 16 * tile + 8, :] = high
        lhs[16 * tile + 8 : 16 * tile + 16, :] = rim[side] - high
    state = [mag[comp] for comp in range(3)]
    for comp in range(3):
        set_lhs(1, state[comp], comp)
    for copy in loads[7:]:
        copy.wait()

    def first_exchange(k, _):
        self_high, self_low = split(tself[k])
        next_high, next_low = split(tnext[k])
        near_high[k] = jnp.concatenate([self_high, next_high], axis=1)
        near_low[k] = jnp.concatenate([self_low, next_low], axis=1)
        above[k] = jnp.concatenate([next_high, next_low], axis=0)
        exchange(k, lhs, near_high, near_low, above, ex)
        return 0

    def next_exchange(k, _):
        exchange(k, lhs, near_high, near_low, above, ex)
        return 0

    lax.fori_loop(0, n_tiles, first_exchange, 0, unroll=4)
    profile = jnp.broadcast_to(prof[...], (8, 128))
    temp = jnp.concatenate(
        [jnp.take_along_axis(profile, tidx[at : at + 8, :], axis=1) for at in range(0, n_tiles, 8)], axis=0
    )
    target = 0.05 + jnp.maximum(1.0 - temp, 0.0)

    def wait_answer(step, _):
        other = lax.rem(track + step, n_track)
        copy = remote(answer.at[other], answered.at[other], ans_send.at[other], ans_recv.at[other], (head, other))
        copy.wait_send()
        copy.wait_recv()
        return 0

    lax.fori_loop(1, n_track, wait_answer, 0)
    table = halves(answered[...].reshape(8 * n_track, 128))
    applied = [[] for _ in range(3)]
    for pair in range(n_tiles // 2):
        found = lookup(table, [addr[2 * pair + i : 2 * pair + i + 1, :] for i in range(2)])
        for value in found:
            for comp in range(3):
                applied[comp].append(value[2 * comp : 2 * comp + 1, :])
    applied = [jnp.concatenate(rows, axis=0) for rows in applied]

    state = llb_section(state, [a + e for a, e in zip(applied, get_ex(ex))], target)
    put_edges(edge_new, state)
    start(rim_copies(n_head, n_track, edge_new, rim_new, rim_new_send, rim_new_recv, False))
    for comp in range(3):
        state_out[comp] = state[comp]
        applied_out[comp] = applied[comp]
    target_out[...] = target

    lhs[0:16, :] = jnp.zeros((16, width), F32)
    lhs[16 * (n_tiles + 1) :, :] = jnp.zeros((16, width), F32)
    for comp in range(3):
        set_lhs(1, state[comp], comp)
    lax.fori_loop(0, EARLY, next_exchange, 0, unroll=4)
    finish(rim_copies(n_head, n_track, edge_new, rim_new, rim_new_send, rim_new_recv, True))


def last_kernel(
    pot, near_high, near_low, above, lhs, ex_early, rim_new, state_in, applied, target,
    relaxed_hbm, magnet_hbm,
    ex, state_out, sem,
):
    n_x, n_y, _ = relaxed_hbm.shape
    n_tiles, width = target.shape
    store = pltpu.make_async_copy(pot.at[pl.ds(1, n_x), pl.ds(ROW0, n_y), :], relaxed_hbm, sem.at[0])
    store.start()
    ex[0 : 8 * EARLY, :] = ex_early[0 : 8 * EARLY, :]

    def next_exchange(k, _):
        exchange(k, lhs, near_high, near_low, above, ex)
        return 0

    lax.fori_loop(EARLY, n_tiles, next_exchange, 0, unroll=4)
    for side, tile in ((0, 0), (1, n_tiles - 1)):
        high = rim_new[side].astype(BF16).astype(F32)
        both = jnp.concatenate([high, rim_new[side] - high], axis=0).astype(BF16)
        if side == 0:
            parts = mxu(both, near_high[tile][:, width:], NT) + mxu(both, near_low[tile][:, width:], NT)
        else:
            parts = mxu(jnp.concatenate([both, both], axis=1), above[tile], NN)
        ex[8 * tile : 8 * tile + 8, :] = ex[8 * tile : 8 * tile + 8, :] + fold(parts)
    state = [state_in[comp] for comp in range(3)]
    fields = [applied[comp] + e for comp, e in enumerate(get_ex(ex))]
    for comp, value in enumerate(llb_section(state, fields, target[...])):
        state_out[comp] = value
    copy = pltpu.make_async_copy(state_out, magnet_hbm, sem.at[1])
    copy.start()
    copy.wait()
    store.wait()


def per_device(n_head, n_track, potential, source, depth_kernel, magnet, footprint, temp_index, temp_profile, self_tiles, next_tiles):
    n_x, n_y, n_z = potential.shape
    n_tiles, width = self_tiles.shape[1], self_tiles.shape[2]
    padded = (n_x + 2, n_y + 16, n_z)
    hbm, vmem, dma = pltpu.HBM, pltpu.VMEM, pltpu.SemaphoreType.DMA
    in_hbm = pl.BlockSpec(memory_space=hbm)
    in_vmem = pl.BlockSpec(memory_space=vmem)
    arguments = (
        potential,
        source,
        depth_kernel,
        magnet.reshape(3, n_tiles, width),
        footprint.reshape(n_tiles, width),
        temp_index.reshape(n_tiles, width),
        temp_profile.reshape(1, -1),
        self_tiles[0],
        next_tiles[0],
    )
    arguments = [pltpu.with_memory_space_constraint(a, hbm) for a in arguments]
    grains = (3, n_tiles, width)
    shared = (
        vmem(padded, F32),
        vmem((n_tiles, width, 2 * width), BF16),
        vmem((n_tiles, width, 2 * width), BF16),
        vmem((n_tiles, 2 * width, width), BF16),
        vmem((16 * (n_tiles + 2), width), F32),
        vmem((8 * n_tiles, width), F32),
        vmem((2, 8, width), F32),
        vmem(grains, F32),
        vmem(grains, F32),
        vmem((n_tiles, width), F32),
    )
    results = pl.pallas_call(
        functools.partial(main_kernel, n_head, n_track),
        out_shape=shared,
        in_specs=[in_hbm] * 9,
        out_specs=(in_vmem,) * len(shared),
        scratch_shapes=[
            vmem(padded, F32),
            vmem((n_x, n_y, n_z), F32),
            vmem((3, n_z), F32),
            vmem(grains, F32),
            vmem((n_tiles, width), I32),
            vmem((n_tiles, width), I32),
            vmem((1, 128), F32),
            vmem((n_tiles, width, width), F32),
            vmem((n_tiles, width, width), F32),
            *[vmem((2, 8, width), F32)] * 3,
            *[vmem((2, n_x, 1, n_z), F32)] * 4,
            vmem((n_tiles, width), I32),
            vmem((n_track, 2, width), I32),
            vmem((n_track, 2, width), I32),
            vmem((8 * (n_x // 2), n_y), F32),
            vmem((n_track, 8, width), F32),
            vmem((n_track, 8, width), F32),
            dma((11,)),
            *[dma((4,))] * 4,
            *[dma((2,))] * 4,
            *[dma((n_track,))] * 4,
        ],
        compiler_params=pltpu.CompilerParams(
            collective_id=0, has_side_effects=True, vmem_limit_bytes=24 << 20
        ),
        name="pole_and_grains",
    )(*arguments)
    relaxed, magnet_out = pl.pallas_call(
        last_kernel,
        out_shape=(hbm(potential.shape, F32), hbm(grains, F32)),
        in_specs=[in_vmem] * len(shared),
        out_specs=(in_hbm, in_hbm),
        scratch_shapes=[vmem((8 * n_tiles, width), F32), vmem(grains, F32), dma((2,))],
        compiler_params=pltpu.CompilerParams(vmem_limit_bytes=4 << 20),
        name="results",
    )(*results)
    return relaxed, magnet_out.reshape(magnet.shape)


def solution(mesh):
    in_specs = (
        P("head", "track", None),
        P("head", "track", None),
        P(),
        P(None, "track", "head"),
        P("track", "head"),
        P("track", "head"),
        P(),
        P("track", "head", None, None),
        P("track", "head", None, None),
    )
    out_specs = (P("head", "track", None), P(None, "track", "head"))
    return jax.shard_map(
        functools.partial(per_device, mesh.shape["head"], mesh.shape["track"]),
        mesh=mesh,
        in_specs=in_specs,
        out_specs=out_specs,
        check_vma=False,
    )
```

```python
import functools

import jax
import jax.numpy as jnp
from jax import lax
from jax.experimental import pallas as pl
from jax.experimental.pallas import tpu as pltpu
from jax.sharding import PartitionSpec as P

F32 = jnp.float32
BF16 = jnp.bfloat16
I32 = jnp.int32
NN = (((1,), (0,)), ((), ()))
NT = (((1,), (1,)), ((), ()))
ROW0 = 8
EARLY = 16


def mxu(a, b, dims):
    return lax.dot_general(a, b, dims, preferred_element_type=F32)


def split(a):
    high = a.astype(BF16)
    return high, (a - high.astype(F32)).astype(BF16)


def face(a, b):
    differ = b - a
    perm = 1.0 + pltpu.reciprocal(0.25 + differ * differ)
    return perm, perm * differ


def one_hot_rows(index, count):
    lanes = index.shape[1]
    rows = lax.broadcasted_iota(I32, (count, lanes), 0)
    return jnp.where(rows == jnp.broadcast_to(index, (count, lanes)), 1.0, 0.0)


def lookup(table, address):
    hot = jnp.concatenate([one_hot_rows(a & 127, 128) for a in address], axis=1).astype(BF16)
    found = mxu(table, jnp.concatenate([hot, hot], axis=0), NN)
    results = []
    for part, a in enumerate(address):
        group = jnp.broadcast_to(a >> 8, (8, 128))
        odd = jnp.broadcast_to((a >> 7) & 1, (8, 128))
        total = jnp.zeros((8, 128), F32)
        for g in range(table.shape[0] // 8):
            total = total + jnp.where(
                group == g, found[8 * g : 8 * g + 8, 128 * part : 128 * part + 128], 0.0
            )
        results.append(jnp.where(odd == 0, total, pltpu.roll(total, 7, 0)))
    return results


def halves(rows):
    high, low = split(rows)
    return jnp.concatenate([high, low], axis=1)


def llb_section(state, field, target):
    mx, my, mz = state
    sq_norm = mx * mx + my * my + mz * mz
    pull = 0.5 * (1.0 - sq_norm / target)
    hx, hy, hz = (f + pull * m for f, m in zip(field, state))
    tx, ty, tz = my * hz - mz * hy, mz * hx - mx * hz, mx * hy - my * hx
    dx, dy, dz = my * tz - mz * ty, mz * tx - mx * tz, mx * ty - my * tx
    along = 0.3 * (mx * hx + my * hy + mz * hz)
    return tuple(
        m + 0.1 * (along * m - t - 0.5 * d)
        for m, t, d in zip(state, (tx, ty, tz), (dx, dy, dz))
    )


def has_neighbours(n_head, n_track):
    head = lax.axis_index("head")
    track = lax.axis_index("track")
    return head, track, head > 0, head < n_head - 1, track > 0, track < n_track - 1


def remote(a, b, send, recv, device):
    return pltpu.make_async_remote_copy(
        src_ref=a, dst_ref=b, send_sem=send, recv_sem=recv, device_id=device,
        device_id_type=pl.DeviceIdType.MESH,
    )


def start(copies):
    for there, copy in copies:

        @pl.when(there)
        def _():
            copy.start()


def finish(copies, sent):
    for there, copy in copies:

        @pl.when(there)
        def _():
            if sent:
                copy.wait_send()
            else:
                copy.wait_recv()


def greet(n_head, n_track):
    head, track, has_low_x, has_high_x, _, _ = has_neighbours(n_head, n_track)
    barrier = pltpu.get_barrier_semaphore()

    def hello(step, _):
        other = (head, lax.rem(track + step, n_track))
        pl.semaphore_signal(barrier, inc=1, device_id=other, device_id_type=pl.DeviceIdType.MESH)
        return 0

    lax.fori_loop(1, n_track, hello, 0)
    for there, other in ((has_low_x, head - 1), (has_high_x, head + 1)):

        @pl.when(there)
        def _():
            pl.semaphore_signal(
                barrier, inc=1, device_id=(other, track), device_id_type=pl.DeviceIdType.MESH
            )

    return barrier, n_track - 1 + has_low_x.astype(I32) + has_high_x.astype(I32)


def rim_copies(n_head, n_track, source, target, send, recv, waits):
    head, track, has_low_x, has_high_x, _, _ = has_neighbours(n_head, n_track)
    low, high = (head - 1, track), (head + 1, track)
    if waits:
        return [
            (has_low_x, remote(source.at[0], target.at[0], send.at[0], recv.at[0], low)),
            (has_high_x, remote(source.at[1], target.at[1], send.at[1], recv.at[1], high)),
        ]
    return [
        (has_low_x, remote(source.at[0], target.at[1], send.at[0], recv.at[1], low)),
        (has_high_x, remote(source.at[1], target.at[0], send.at[1], recv.at[0], high)),
    ]


def put_edges(edge, sides):
    edge[...] = jnp.zeros(edge.shape, F32)
    for comp in range(3):
        low, high = sides[0][comp], sides[1][comp]
        last = high.shape[0] - 1
        edge[0, comp : comp + 1, :] = low[0:1, :]
        edge[1, comp : comp + 1, :] = high[last : last + 1, :]


def rank_grains(foot, addr, ask, n_track):
    later = lax.broadcasted_iota(I32, (128, 128), 0) < lax.broadcasted_iota(I32, (128, 128), 1)
    count_matrix = jnp.concatenate(
        [jnp.where(later, 1.0, 0.0), jnp.ones((128, 128), F32)], axis=1
    ).astype(BF16)
    before = jnp.zeros((n_track, 128), F32)
    asks = jnp.zeros((128, 128), F32)
    for chunk in range(foot.shape[0]):
        cell = foot[chunk : chunk + 1, :]
        owner = cell >> 13
        hot = one_hot_rows(owner, n_track)
        counts = mxu(hot.astype(BF16), count_matrix, NN)
        place = jnp.sum(hot * (counts[:, :128] + before), axis=0, keepdims=True).astype(I32)
        before = before + counts[:, 128:]
        where_at = owner * 256 + place
        addr[chunk : chunk + 1, :] = where_at
        row = one_hot_rows(where_at >> 7, 2 * n_track)
        lane = one_hot_rows(where_at & 127, 128)
        high = jnp.broadcast_to((cell >> 7) & 63, row.shape).astype(F32)
        low = jnp.broadcast_to(cell & 127, row.shape).astype(F32)
        values = jnp.concatenate([row * high, row * low], axis=0)
        asks = asks + mxu(values.astype(BF16), lane.astype(BF16), NT)
    cells = (asks[: 2 * n_track] * 128.0 + asks[2 * n_track :]).astype(I32)
    for owner in range(n_track):
        ask[owner, 0:2, :] = cells[2 * owner : 2 * owner + 2, :]


def swept(source, src, faces, slot, x, row, rows_at, carried):
    lanes = lax.broadcasted_iota(I32, (rows_at, 128), 1)
    o = ROW0 + row
    center = source[x + 1, o : o + rows_at, :]
    depth = center.shape[1]
    perm, flux = face(center, source[x + 2, o : o + rows_at, :])
    numer = (src[x, row : row + rows_at, :] - carried[1]) + flux
    denom = (1.0 + carried[0]) + perm
    carried = (perm, flux)
    perm, flux = face(source[x + 1, o - 1 : o - 1 + rows_at, :], center)
    faces[0, slot, 0:rows_at, :] = perm
    faces[1, slot, 0:rows_at, :] = flux
    numer = numer - flux
    denom = denom + perm
    end = o + rows_at
    perm, flux = face(source[x + 1, end - 1 : end, :], source[x + 1, end : end + 1, :])
    faces[0, slot, rows_at : rows_at + 1, :] = perm
    faces[1, slot, rows_at : rows_at + 1, :] = flux
    for other in (
        jnp.where(lanes == depth - 1, 0.0, pltpu.roll(center, depth - 1, 1)),
        jnp.where(lanes == 0, 0.0, pltpu.roll(center, 1, 1)),
    ):
        perm, flux = face(center, other)
        numer = numer + flux
        denom = denom + perm
    numer = numer + faces[1, slot, 1 : rows_at + 1, :]
    denom = denom + faces[0, slot, 1 : rows_at + 1, :]
    return center + (0.8 * numer) * pltpu.reciprocal(denom), carried


def fold(parts):
    return parts[:8] + parts[8:]


def exchange(k, lhs, near_high, near_low, above, ex):
    def get_lhs(tile):
        return lhs[pl.ds(pl.multiple_of(16 * tile, 16), 16), :].astype(BF16)

    near = jnp.concatenate([get_lhs(k + 1), get_lhs(k)], axis=1)
    far = get_lhs(k + 2)
    parts = mxu(near, near_high[k], NT) + mxu(near, near_low[k], NT)
    parts = parts + mxu(jnp.concatenate([far, far], axis=1), above[k], NN)
    ex[pl.ds(pl.multiple_of(8 * k, 8), 8), :] = fold(parts)


def get_ex(ex):
    return [ex[pl.ds(comp, ex.shape[0] // 8, stride=8), :] for comp in range(3)]


def main_kernel(
    n_head, n_track,
    pot_hbm, src_hbm, dk_hbm, mag_hbm, foot_hbm, temp_hbm, prof_hbm, self_hbm, next_hbm,
    pot, near_high, near_low, above, lhs, ex, rim_new, state_out, applied_out, target_out,
    mid, src, faces, dk, mag, foot, tidx, prof, tself, tnext,
    rim, edge, edge_new, lines, lines_in, lines_mid, lines_mid_in,
    addr, ask, asked, surf, answer, answered,
    in_sem, halo_send, halo_recv, mid_send, mid_recv, rim_send, rim_recv,
    rim_new_send, rim_new_recv, ask_send, ask_recv, ans_send, ans_recv,
):
    head, track, has_low_x, has_high_x, has_low_y, has_high_y = has_neighbours(n_head, n_track)
    n_x, n_y, n_z = src.shape
    n_tiles, width = mag.shape[1:]
    inner, all_x = pl.ds(ROW0, n_y), pl.ds(1, n_x)
    low_x, high_x = (head - 1, track), (head + 1, track)
    low_y, high_y = (head, track - 1), (head, track + 1)
    rows8 = lax.broadcasted_iota(I32, (8, 128), 0)

    barrier, n_greeted = greet(n_head, n_track)
    pairs = [
        (foot_hbm, foot),
        (mag_hbm, mag),
        (pot_hbm.at[:, pl.ds(0, 1), :], lines.at[0]),
        (pot_hbm.at[:, pl.ds(n_y - 1, 1), :], lines.at[1]),
        (pot_hbm, pot.at[all_x, inner, :]),
        (src_hbm, src),
        (dk_hbm, dk),
        (temp_hbm, tidx),
        (prof_hbm, prof),
        (self_hbm, tself),
        (next_hbm, tnext),
    ]
    loads = [pltpu.make_async_copy(a, b, in_sem.at[i]) for i, (a, b) in enumerate(pairs)]
    for copy in loads:
        copy.start()

    for side, there in enumerate((has_low_x, has_high_x)):

        @pl.when(jnp.logical_not(there))
        def _():
            for ref in (pot, mid):
                ref[side * (n_x + 1), ROW0 : ROW0 + n_y, :] = jnp.zeros((n_y, n_z), F32)
            for ref in (rim, rim_new):
                ref[side] = jnp.zeros(ref.shape[1:], F32)

    for side, there in enumerate((has_low_y, has_high_y)):

        @pl.when(jnp.logical_not(there))
        def _():
            for ref in (lines_in, lines_mid_in):
                ref[side] = jnp.zeros(ref.shape[1:], F32)

    loads[0].wait()
    rank_grains(foot, addr, ask, n_track)
    asked[track] = ask[track]
    loads[1].wait()
    put_edges(edge, [[mag[comp] for comp in range(3)]] * 2)
    loads[2].wait()
    loads[3].wait()
    pl.semaphore_wait(barrier, n_greeted)

    def halo(planes, rows, target, rows_in, send, recv):
        return [
            (has_low_x, remote(planes[0], target.at[n_x + 1, inner, :], send.at[0], recv.at[1], low_x)),
            (has_high_x, remote(planes[1], target.at[0, inner, :], send.at[1], recv.at[0], high_x)),
            (has_low_y, remote(rows.at[0], rows_in.at[1], send.at[2], recv.at[3], low_y)),
            (has_high_y, remote(rows.at[1], rows_in.at[0], send.at[3], recv.at[2], high_y)),
        ]

    def halo_waits(planes, rows, target, rows_in, send, recv):
        return [
            (has_low_x, remote(planes[0], target.at[0, inner, :], send.at[0], recv.at[0], low_x)),
            (has_high_x, remote(planes[1], target.at[n_x + 1, inner, :], send.at[1], recv.at[1], high_x)),
            (has_low_y, remote(rows.at[0], rows_in.at[0], send.at[2], recv.at[2], low_y)),
            (has_high_y, remote(rows.at[1], rows_in.at[1], send.at[3], recv.at[3], high_y)),
        ]

    def place_lines(rows_in, target):
        target[1 : n_x + 1, ROW0 - 1 : ROW0, :] = rows_in[0]
        target[1 : n_x + 1, ROW0 + n_y : ROW0 + n_y + 1, :] = rows_in[1]

    start_halo = [pot_hbm.at[0], pot_hbm.at[n_x - 1]], lines, pot, lines_in, halo_send, halo_recv
    start(halo(*start_halo))

    def send_ask(step, _):
        other = lax.rem(track + step, n_track)
        remote(ask.at[other], asked.at[track], ask_send.at[other], ask_recv.at[track], (head, other)).start()
        return 0

    lax.fori_loop(1, n_track, send_ask, 0)
    start(rim_copies(n_head, n_track, edge, rim, rim_send, rim_recv, False))
    loads[4].wait()
    loads[5].wait()

    edge_rows = 32

    def sweep_chunk(source, target, row, rows_at, unroll, beside=None):
        rows = slice(ROW0 + row, ROW0 + row + rows_at)

        def planes(base, count, carried):
            for j in range(count):
                target[base + j + 1, rows, :], carried = swept(source, src, faces, j, base + j, row, rows_at, carried)
            return carried

        def trip(i, carried):
            if beside is not None:
                beside(i)
            return planes(1 + unroll * i, unroll, carried)

        trips = (n_x - 2) // unroll
        carried = planes(1, unroll, face(source[1, rows, :], source[2, rows, :]))
        carried = lax.fori_loop(1, trips, trip, carried)
        if beside is not None:
            beside(trips)
        planes(1 + unroll * trips, n_x - 2 - unroll * trips, carried)

    def sweep_inner(source, target):
        sweep_chunk(source, target, edge_rows, n_y - 2 * edge_rows, 4)

    def sweep_outer(source, target):
        for side, x in enumerate((0, n_x - 1)):
            for row in range(0, n_y, edge_rows):
                rows = slice(ROW0 + row, ROW0 + row + edge_rows)
                carried = face(source[x, rows, :], source[x + 1, rows, :])
                slot = 4 * side + row // edge_rows
                target[x + 1, rows, :], _ = swept(source, src, faces, slot, x, row, edge_rows, carried)

    def sweep_edge(source, target, row, beside=None):
        sweep_chunk(source, target, row, edge_rows, 8, beside)

    sweep_inner(pot, mid)
    finish(halo_waits(*start_halo), False)
    place_lines(lines_in, pot)
    sweep_outer(pot, mid)
    mid_halo = [mid.at[1, inner, :], mid.at[n_x, inner, :]], lines_mid, mid, lines_mid_in, mid_send, mid_recv
    sends = halo(*mid_halo)
    start(sends[:2])
    for row in (0, n_y - edge_rows):
        sweep_edge(pot, mid, row)
    lines_mid[0] = mid[1 : n_x + 1, ROW0 : ROW0 + 1, :]
    lines_mid[1] = mid[1 : n_x + 1, ROW0 + n_y - 1 : ROW0 + n_y, :]
    start(sends[2:])

    sweep_inner(mid, pot)
    loads[6].wait()
    kernels = []
    for odd in range(2):
        weights = jnp.zeros((8, 128), F32)
        for comp in range(3):
            weights = weights + jnp.where(
                rows8 == 2 * comp + odd, jnp.broadcast_to(dk[comp : comp + 1, :], (8, 128)), 0.0
            )
        high = weights.astype(BF16).astype(F32)
        kernels.append(jnp.concatenate([high, weights - high], axis=0))
    kernels = jnp.concatenate(kernels, axis=0).astype(BF16)
    kernels = jnp.concatenate([kernels, kernels], axis=1)

    def surface(i):
        for j in range(4):
            at = 4 * (i - 1) + j
            both = [halves(pot[2 * at + odd + 1, ROW0 : ROW0 + n_y, :]) for odd in range(2)]
            found = mxu(kernels, jnp.concatenate(both, axis=0), NT)
            total = (found[0:8, :n_y] + found[8:16, :n_y]) + (found[16:24, n_y:] + found[24:32, n_y:])
            surf[pl.ds(8 * at if isinstance(at, int) else pl.multiple_of(8 * at, 8), 8), :] = total

    finish(halo_waits(*mid_halo), False)
    place_lines(lines_mid_in, mid)
    sweep_outer(mid, pot)
    sweep_edge(mid, pot, 0)
    sweep_edge(mid, pot, n_y - edge_rows, surface)
    surface(n_x // 8)

    def wait_ask(step, _):
        other = lax.rem(track + step, n_track)
        remote(ask.at[other], asked.at[other], ask_send.at[other], ask_recv.at[other], (head, other)).wait_recv()
        return 0

    lax.fori_loop(1, n_track, wait_ask, 0)
    table = halves(surf[...])

    def reply(far_y, own):
        y, z, x = track // 8, (track // 4) % 2, track % 4
        others = [
            (y + far_y) % 4 * 8 + (z + far_z) % 2 * 4 + (x + far_x) % 4
            for far_z in (1, 0)
            for far_x in (2, 1, 3, 0)
        ]
        for other in others:
            low, high = lookup(table, [asked[other, 0:1, :], asked[other, 1:2, :]])
            answer[other] = jnp.where(rows8 % 2 == 0, low, pltpu.roll(high, 1, 0))
        if own:
            answered[track] = answer[track]
            others = others[:-1]
        for other in others:
            remote(answer.at[other], answered.at[track], ans_send.at[other], ans_recv.at[track], (head, other)).start()

    def reply_far(group, _):
        reply(jnp.where(group == 0, 2, jnp.where(group == 1, 1, 3)), False)
        return 0

    lax.fori_loop(0, 3, reply_far, 0)
    reply(0, True)

    def set_lhs(tile, value, comp):
        high = value.astype(BF16).astype(F32)
        lhs[pl.ds(16 * tile + comp, value.shape[0], stride=16), :] = high
        lhs[pl.ds(16 * tile + 8 + comp, value.shape[0], stride=16), :] = value - high

    lhs[...] = jnp.zeros(lhs.shape, F32)
    finish(rim_copies(n_head, n_track, edge, rim, rim_send, rim_recv, True), False)
    for side, tile in ((0, 0), (1, n_tiles + 1)):
        high = rim[side].astype(BF16).astype(F32)
        lhs[16 * tile : 16 * tile + 8, :] = high
        lhs[16 * tile + 8 : 16 * tile + 16, :] = rim[side] - high
    state = [mag[comp] for comp in range(3)]
    for comp in range(3):
        set_lhs(1, state[comp], comp)
    for copy in loads[7:]:
        copy.wait()

    def first_exchange(k, _):
        self_high, self_low = split(tself[k])
        next_high, next_low = split(tnext[k])
        near_high[k] = jnp.concatenate([self_high, next_high], axis=1)
        near_low[k] = jnp.concatenate([self_low, next_low], axis=1)
        above[k] = jnp.concatenate([next_high, next_low], axis=0)
        exchange(k, lhs, near_high, near_low, above, ex)
        return 0

    def next_exchange(k, _):
        exchange(k, lhs, near_high, near_low, above, ex)
        return 0

    lax.fori_loop(0, n_tiles, first_exchange, 0, unroll=4)
    profile = jnp.broadcast_to(prof[...], (8, 128))
    temp = jnp.concatenate(
        [jnp.take_along_axis(profile, tidx[at : at + 8, :], axis=1) for at in range(0, n_tiles, 8)], axis=0
    )
    target = 0.05 + jnp.maximum(1.0 - temp, 0.0)

    def wait_answer(step, _):
        other = lax.rem(track + step, n_track)
        remote(answer.at[other], answered.at[other], ans_send.at[other], ans_recv.at[other], (head, other)).wait_recv()
        return 0

    lax.fori_loop(1, n_track, wait_answer, 0)
    table = halves(answered[...].reshape(8 * n_track, 128))
    applied = [[None] * n_tiles for _ in range(3)]

    def find(pair):
        found = lookup(table, [addr[2 * pair + i : 2 * pair + i + 1, :] for i in range(2)])
        for i, value in enumerate(found):
            for comp in range(3):
                applied[comp][2 * pair + i] = value[2 * comp : 2 * comp + 1, :]

    last_pair = n_tiles // 2 - 1
    find(0)
    find(last_pair)
    exs = get_ex(ex)
    blank = jnp.zeros((6, width), F32)
    sides = []
    for rows, order in ((slice(0, 8), (0, 1, None)), (slice(n_tiles - 8, n_tiles), (None, n_tiles - 2, n_tiles - 1))):
        fields = [
            jnp.concatenate([blank if at is None else applied[comp][at] for at in order], axis=0) + exs[comp][rows]
            for comp in range(3)
        ]
        sides.append(llb_section([m[rows] for m in state], fields, target[rows]))
    put_edges(edge_new, sides)
    start(rim_copies(n_head, n_track, edge_new, rim_new, rim_new_send, rim_new_recv, False))
    for pair in range(1, last_pair):
        find(pair)
    applied = [jnp.concatenate(rows, axis=0) for rows in applied]
    state = llb_section(state, [a + e for a, e in zip(applied, exs)], target)
    for comp in range(3):
        state_out[comp] = state[comp]
        applied_out[comp] = applied[comp]
    target_out[...] = target

    lhs[0:16, :] = jnp.zeros((16, width), F32)
    lhs[16 * (n_tiles + 1) :, :] = jnp.zeros((16, width), F32)
    for comp in range(3):
        set_lhs(1, state[comp], comp)
    lax.fori_loop(0, EARLY, next_exchange, 0, unroll=4)

    def wait_sent(step, _):
        other = lax.rem(track + step, n_track)
        remote(ask.at[other], asked.at[other], ask_send.at[other], ask_recv.at[other], (head, other)).wait_send()
        remote(answer.at[other], answered.at[other], ans_send.at[other], ans_recv.at[other], (head, other)).wait_send()
        return 0

    lax.fori_loop(1, n_track, wait_sent, 0)
    finish(halo_waits(*start_halo), True)
    finish(halo_waits(*mid_halo), True)
    finish(rim_copies(n_head, n_track, edge, rim, rim_send, rim_recv, True), True)
    new_rim = rim_copies(n_head, n_track, edge_new, rim_new, rim_new_send, rim_new_recv, True)
    finish(new_rim, True)
    finish(new_rim, False)


def last_kernel(
    pot, near_high, near_low, above, lhs, ex_early, rim_new, state_in, applied, target,
    relaxed_hbm, magnet_hbm,
    ex, state_out, sem,
):
    n_x, n_y, _ = relaxed_hbm.shape
    n_tiles, width = target.shape
    store = pltpu.make_async_copy(pot.at[pl.ds(1, n_x), pl.ds(ROW0, n_y), :], relaxed_hbm, sem.at[0])
    store.start()
    ex[0 : 8 * EARLY, :] = ex_early[0 : 8 * EARLY, :]

    def next_exchange(k, _):
        exchange(k, lhs, near_high, near_low, above, ex)
        return 0

    lax.fori_loop(EARLY, n_tiles, next_exchange, 0, unroll=4)
    for side, tile in ((0, 0), (1, n_tiles - 1)):
        high = rim_new[side].astype(BF16).astype(F32)
        both = jnp.concatenate([high, rim_new[side] - high], axis=0).astype(BF16)
        if side == 0:
            parts = mxu(both, near_high[tile][:, width:], NT) + mxu(both, near_low[tile][:, width:], NT)
        else:
            parts = mxu(jnp.concatenate([both, both], axis=1), above[tile], NN)
        ex[8 * tile : 8 * tile + 8, :] = ex[8 * tile : 8 * tile + 8, :] + fold(parts)
    state = [state_in[comp] for comp in range(3)]
    fields = [applied[comp] + e for comp, e in enumerate(get_ex(ex))]
    for comp, value in enumerate(llb_section(state, fields, target[...])):
        state_out[comp] = value
    copy = pltpu.make_async_copy(state_out, magnet_hbm, sem.at[1])
    copy.start()
    copy.wait()
    store.wait()


def per_device(n_head, n_track, potential, source, depth_kernel, magnet, footprint, temp_index, temp_profile, self_tiles, next_tiles):
    n_x, n_y, n_z = potential.shape
    n_tiles, width = self_tiles.shape[1], self_tiles.shape[2]
    padded = (n_x + 2, n_y + 16, n_z)
    hbm, vmem, dma = pltpu.HBM, pltpu.VMEM, pltpu.SemaphoreType.DMA
    in_hbm = pl.BlockSpec(memory_space=hbm)
    in_vmem = pl.BlockSpec(memory_space=vmem)
    arguments = (
        potential,
        source,
        depth_kernel,
        magnet.reshape(3, n_tiles, width),
        footprint.reshape(n_tiles, width),
        temp_index.reshape(n_tiles, width),
        temp_profile.reshape(1, -1),
        self_tiles[0],
        next_tiles[0],
    )
    arguments = [pltpu.with_memory_space_constraint(a, hbm) for a in arguments]
    grains = (3, n_tiles, width)
    shared = (
        vmem(padded, F32),
        vmem((n_tiles, width, 2 * width), BF16),
        vmem((n_tiles, width, 2 * width), BF16),
        vmem((n_tiles, 2 * width, width), BF16),
        vmem((16 * (n_tiles + 2), width), F32),
        vmem((8 * n_tiles, width), F32),
        vmem((2, 8, width), F32),
        vmem(grains, F32),
        vmem(grains, F32),
        vmem((n_tiles, width), F32),
    )
    results = pl.pallas_call(
        functools.partial(main_kernel, n_head, n_track),
        out_shape=shared,
        in_specs=[in_hbm] * 9,
        out_specs=(in_vmem,) * len(shared),
        scratch_shapes=[
            vmem(padded, F32),
            vmem((n_x, n_y, n_z), F32),
            vmem((2, 8, n_y, n_z), F32),
            vmem((3, n_z), F32),
            vmem(grains, F32),
            vmem((n_tiles, width), I32),
            vmem((n_tiles, width), I32),
            vmem((1, 128), F32),
            vmem((n_tiles, width, width), F32),
            vmem((n_tiles, width, width), F32),
            *[vmem((2, 8, width), F32)] * 3,
            *[vmem((2, n_x, 1, n_z), F32)] * 4,
            vmem((n_tiles, width), I32),
            vmem((n_track, 2, width), I32),
            vmem((n_track, 2, width), I32),
            vmem((8 * (n_x // 2), n_y), F32),
            vmem((n_track, 8, width), F32),
            vmem((n_track, 8, width), F32),
            dma((11,)),
            *[dma((4,))] * 4,
            *[dma((2,))] * 4,
            *[dma((n_track,))] * 4,
        ],
        compiler_params=pltpu.CompilerParams(
            collective_id=0, has_side_effects=True, vmem_limit_bytes=24 << 20
        ),
        name="pole_and_grains",
    )(*arguments)
    relaxed, magnet_out = pl.pallas_call(
        last_kernel,
        out_shape=(hbm(potential.shape, F32), hbm(grains, F32)),
        in_specs=[in_vmem] * len(shared),
        out_specs=(in_hbm, in_hbm),
        scratch_shapes=[vmem((8 * n_tiles, width), F32), vmem(grains, F32), dma((2,))],
        compiler_params=pltpu.CompilerParams(vmem_limit_bytes=4 << 20),
        name="results",
    )(*results)
    return relaxed, magnet_out.reshape(magnet.shape)


def solution(mesh):
    in_specs = (
        P("head", "track", None),
        P("head", "track", None),
        P(),
        P(None, "track", "head"),
        P("track", "head"),
        P("track", "head"),
        P(),
        P("track", "head", None, None),
        P("track", "head", None, None),
    )
    out_specs = (P("head", "track", None), P(None, "track", "head"))
    return jax.shard_map(
        functools.partial(per_device, mesh.shape["head"], mesh.shape["track"]),
        mesh=mesh,
        in_specs=in_specs,
        out_specs=out_specs,
        check_vma=False,
    )
```

```python
import functools

import jax
import jax.numpy as jnp
from jax import lax
from jax.experimental import pallas as pl
from jax.experimental.pallas import tpu as pltpu
from jax.sharding import PartitionSpec as P

F32 = jnp.float32
BF16 = jnp.bfloat16
I32 = jnp.int32
NN = (((1,), (0,)), ((), ()))
NT = (((1,), (1,)), ((), ()))
ROW0 = 8
PARTS = 4
EARLY = 16


def mxu(a, b, dims):
    return lax.dot_general(a, b, dims, preferred_element_type=F32)


def split(a):
    high = a.astype(BF16)
    return high, (a - high.astype(F32)).astype(BF16)


def face(a, b):
    differ = b - a
    perm = 1.0 + pltpu.reciprocal(0.25 + differ * differ)
    return perm, perm * differ


def one_hot_rows(index, count):
    lanes = index.shape[1]
    rows = lax.broadcasted_iota(I32, (count, lanes), 0)
    return jnp.where(rows == jnp.broadcast_to(index, (count, lanes)), 1.0, 0.0)


def lookup(table, address):
    hot = jnp.concatenate([one_hot_rows(a & 127, 128) for a in address], axis=1).astype(BF16)
    found = mxu(table, jnp.concatenate([hot, hot], axis=0), NN)
    results = []
    for part, a in enumerate(address):
        group = jnp.broadcast_to(a >> 8, (8, 128))
        odd = jnp.broadcast_to((a >> 7) & 1, (8, 128))
        total = jnp.zeros((8, 128), F32)
        for g in range(table.shape[0] // 8):
            total = total + jnp.where(
                group == g, found[8 * g : 8 * g + 8, 128 * part : 128 * part + 128], 0.0
            )
        results.append(jnp.where(odd == 0, total, pltpu.roll(total, 7, 0)))
    return results


def halves(rows):
    high, low = split(rows)
    return jnp.concatenate([high, low], axis=1)


def llb_section(state, field, target):
    mx, my, mz = state
    sq_norm = mx * mx + my * my + mz * mz
    pull = 0.5 * (1.0 - sq_norm / target)
    hx, hy, hz = (f + pull * m for f, m in zip(field, state))
    tx, ty, tz = my * hz - mz * hy, mz * hx - mx * hz, mx * hy - my * hx
    dx, dy, dz = my * tz - mz * ty, mz * tx - mx * tz, mx * ty - my * tx
    along = 0.3 * (mx * hx + my * hy + mz * hz)
    return tuple(
        m + 0.1 * (along * m - t - 0.5 * d)
        for m, t, d in zip(state, (tx, ty, tz), (dx, dy, dz))
    )


def has_neighbours(n_head, n_track):
    head = lax.axis_index("head")
    track = lax.axis_index("track")
    return head, track, head > 0, head < n_head - 1, track > 0, track < n_track - 1


def remote(a, b, send, recv, device):
    return pltpu.make_async_remote_copy(
        src_ref=a, dst_ref=b, send_sem=send, recv_sem=recv, device_id=device,
        device_id_type=pl.DeviceIdType.MESH,
    )


def start(copies):
    for there, copy in copies:

        @pl.when(there)
        def _():
            copy.start()


def finish(copies, sent):
    for there, copy in copies:

        @pl.when(there)
        def _():
            if sent:
                copy.wait_send()
            else:
                copy.wait_recv()


def greet(n_head, n_track):
    head, track, has_low_x, has_high_x, _, _ = has_neighbours(n_head, n_track)
    barrier = pltpu.get_barrier_semaphore()

    def hello(step, _):
        other = (head, lax.rem(track + step, n_track))
        pl.semaphore_signal(barrier, inc=1, device_id=other, device_id_type=pl.DeviceIdType.MESH)
        return 0

    lax.fori_loop(1, n_track, hello, 0)
    for there, other in ((has_low_x, head - 1), (has_high_x, head + 1)):

        @pl.when(there)
        def _():
            pl.semaphore_signal(
                barrier, inc=1, device_id=(other, track), device_id_type=pl.DeviceIdType.MESH
            )

    return barrier, n_track - 1 + has_low_x.astype(I32) + has_high_x.astype(I32)


def rim_copies(n_head, n_track, source, target, send, recv, waits):
    head, track, has_low_x, has_high_x, _, _ = has_neighbours(n_head, n_track)
    low, high = (head - 1, track), (head + 1, track)
    if waits:
        return [
            (has_low_x, remote(source.at[0], target.at[0], send.at[0], recv.at[0], low)),
            (has_high_x, remote(source.at[1], target.at[1], send.at[1], recv.at[1], high)),
        ]
    return [
        (has_low_x, remote(source.at[0], target.at[1], send.at[0], recv.at[1], low)),
        (has_high_x, remote(source.at[1], target.at[0], send.at[1], recv.at[0], high)),
    ]


def put_edges(edge, sides):
    edge[...] = jnp.zeros(edge.shape, F32)
    for comp in range(3):
        low, high = sides[0][comp], sides[1][comp]
        last = high.shape[0] - 1
        edge[0, comp : comp + 1, :] = low[0:1, :]
        edge[1, comp : comp + 1, :] = high[last : last + 1, :]


def rank_grains(foot, addr, ask, n_track):
    later = lax.broadcasted_iota(I32, (128, 128), 0) < lax.broadcasted_iota(I32, (128, 128), 1)
    count_matrix = jnp.concatenate(
        [jnp.where(later, 1.0, 0.0), jnp.ones((128, 128), F32)], axis=1
    ).astype(BF16)
    before = jnp.zeros((n_track, 128), F32)
    asks = jnp.zeros((128, 128), F32)
    for chunk in range(foot.shape[0]):
        cell = foot[chunk : chunk + 1, :]
        owner = cell >> 13
        hot = one_hot_rows(owner, n_track)
        counts = mxu(hot.astype(BF16), count_matrix, NN)
        place = jnp.sum(hot * (counts[:, :128] + before), axis=0, keepdims=True).astype(I32)
        before = before + counts[:, 128:]
        where_at = owner * 256 + place
        addr[chunk : chunk + 1, :] = where_at
        row = one_hot_rows(where_at >> 7, 2 * n_track)
        lane = one_hot_rows(where_at & 127, 128)
        high = jnp.broadcast_to((cell >> 7) & 63, row.shape).astype(F32)
        low = jnp.broadcast_to(cell & 127, row.shape).astype(F32)
        values = jnp.concatenate([row * high, row * low], axis=0)
        asks = asks + mxu(values.astype(BF16), lane.astype(BF16), NT)
    cells = (asks[: 2 * n_track] * 128.0 + asks[2 * n_track :]).astype(I32)
    for owner in range(n_track):
        ask[owner, 0:2, :] = cells[2 * owner : 2 * owner + 2, :]


def swept(source, src, faces, slot, x, row, rows_at, carried):
    lanes = lax.broadcasted_iota(I32, (rows_at, 128), 1)
    o = ROW0 + row
    center = source[x + 1, o : o + rows_at, :]
    depth = center.shape[1]
    perm, flux = face(center, source[x + 2, o : o + rows_at, :])
    numer = (src[x, row : row + rows_at, :] - carried[1]) + flux
    denom = (1.0 + carried[0]) + perm
    carried = (perm, flux)
    perm, flux = face(source[x + 1, o - 1 : o - 1 + rows_at, :], center)
    faces[0, slot, 0:rows_at, :] = perm
    faces[1, slot, 0:rows_at, :] = flux
    numer = numer - flux
    denom = denom + perm
    end = o + rows_at
    perm, flux = face(source[x + 1, end - 1 : end, :], source[x + 1, end : end + 1, :])
    faces[0, slot, rows_at : rows_at + 1, :] = perm
    faces[1, slot, rows_at : rows_at + 1, :] = flux
    for other in (
        jnp.where(lanes == depth - 1, 0.0, pltpu.roll(center, depth - 1, 1)),
        jnp.where(lanes == 0, 0.0, pltpu.roll(center, 1, 1)),
    ):
        perm, flux = face(center, other)
        numer = numer + flux
        denom = denom + perm
    numer = numer + faces[1, slot, 1 : rows_at + 1, :]
    denom = denom + faces[0, slot, 1 : rows_at + 1, :]
    return center + (0.8 * numer) * pltpu.reciprocal(denom), carried


def fold(parts):
    return parts[:8] + parts[8:]


def exchange(k, lhs, near_high, near_low, above, ex):
    def get_lhs(tile):
        return lhs[pl.ds(pl.multiple_of(16 * tile, 16), 16), :].astype(BF16)

    near = jnp.concatenate([get_lhs(k + 1), get_lhs(k)], axis=1)
    far = get_lhs(k + 2)
    parts = mxu(near, near_high[k], NT) + mxu(near, near_low[k], NT)
    parts = parts + mxu(jnp.concatenate([far, far], axis=1), above[k], NN)
    ex[pl.ds(pl.multiple_of(8 * k, 8), 8), :] = fold(parts)


def get_ex(ex):
    return [ex[pl.ds(comp, ex.shape[0] // 8, stride=8), :] for comp in range(3)]


def main_kernel(
    n_head, n_track,
    pot_hbm, src_hbm, dk_hbm, mag_hbm, foot_hbm, temp_hbm, prof_hbm, self_hbm, next_hbm,
    pot, near_high, near_low, above, lhs, ex, rim_new, state_out, applied_out, target_out,
    mid, src, faces, dk, mag, foot, tidx, prof, tself, tnext,
    rim, edge, edge_new, lines, lines_in, lines_mid, lines_mid_in,
    addr, ask, asked, surf, answer, answered,
    in_sem, halo_send, halo_recv, mid_send, mid_recv, rim_send, rim_recv,
    rim_new_send, rim_new_recv, ask_send, ask_recv, ans_send, ans_recv,
):
    head, track, has_low_x, has_high_x, has_low_y, has_high_y = has_neighbours(n_head, n_track)
    n_x, n_y, n_z = src.shape
    n_tiles, width = mag.shape[1:]
    inner, all_x = pl.ds(ROW0, n_y), pl.ds(1, n_x)
    low_x, high_x = (head - 1, track), (head + 1, track)
    low_y, high_y = (head, track - 1), (head, track + 1)
    rows8 = lax.broadcasted_iota(I32, (8, 128), 0)

    barrier, n_greeted = greet(n_head, n_track)
    part = n_x // PARTS
    parts = range(0, n_x, part)
    pairs = [
        (foot_hbm, foot),
        (mag_hbm, mag),
        (pot_hbm.at[:, pl.ds(0, 1), :], lines.at[0]),
        (pot_hbm.at[:, pl.ds(n_y - 1, 1), :], lines.at[1]),
        *[(pot_hbm.at[pl.ds(x, part), :, :], pot.at[pl.ds(x + 1, part), inner, :]) for x in parts],
        *[(src_hbm.at[pl.ds(x, part), :, :], src.at[pl.ds(x, part), :, :]) for x in parts],
        (dk_hbm, dk),
        (temp_hbm, tidx),
        (prof_hbm, prof),
        (self_hbm, tself),
        (next_hbm, tnext),
    ]
    loads = [pltpu.make_async_copy(a, b, in_sem.at[i]) for i, (a, b) in enumerate(pairs)]
    large = loads[4 : 4 + 2 * PARTS]
    small = loads[4 + 2 * PARTS : -2]
    for copy in loads[:-2]:
        copy.start()

    for side, there in enumerate((has_low_x, has_high_x)):

        @pl.when(jnp.logical_not(there))
        def _():
            for ref in (pot, mid):
                ref[side * (n_x + 1), ROW0 : ROW0 + n_y, :] = jnp.zeros((n_y, n_z), F32)
            for ref in (rim, rim_new):
                ref[side] = jnp.zeros(ref.shape[1:], F32)

    for side, there in enumerate((has_low_y, has_high_y)):

        @pl.when(jnp.logical_not(there))
        def _():
            for ref in (lines_in, lines_mid_in):
                ref[side] = jnp.zeros(ref.shape[1:], F32)

    loads[0].wait()
    rank_grains(foot, addr, ask, n_track)
    asked[track] = ask[track]
    loads[1].wait()
    put_edges(edge, [[mag[comp] for comp in range(3)]] * 2)
    loads[2].wait()
    loads[3].wait()
    pl.semaphore_wait(barrier, n_greeted)

    def halo(planes, rows, target, rows_in, send, recv):
        return [
            (has_low_x, remote(planes[0], target.at[n_x + 1, inner, :], send.at[0], recv.at[1], low_x)),
            (has_high_x, remote(planes[1], target.at[0, inner, :], send.at[1], recv.at[0], high_x)),
            (has_low_y, remote(rows.at[0], rows_in.at[1], send.at[2], recv.at[3], low_y)),
            (has_high_y, remote(rows.at[1], rows_in.at[0], send.at[3], recv.at[2], high_y)),
        ]

    def halo_waits(planes, rows, target, rows_in, send, recv):
        return [
            (has_low_x, remote(planes[0], target.at[0, inner, :], send.at[0], recv.at[0], low_x)),
            (has_high_x, remote(planes[1], target.at[n_x + 1, inner, :], send.at[1], recv.at[1], high_x)),
            (has_low_y, remote(rows.at[0], rows_in.at[0], send.at[2], recv.at[2], low_y)),
            (has_high_y, remote(rows.at[1], rows_in.at[1], send.at[3], recv.at[3], high_y)),
        ]

    def place_lines(rows_in, target):
        target[1 : n_x + 1, ROW0 - 1 : ROW0, :] = rows_in[0]
        target[1 : n_x + 1, ROW0 + n_y : ROW0 + n_y + 1, :] = rows_in[1]

    everyone = pl.ds(0, n_track - 1)
    next_one = (head, lax.rem(track + 1, n_track))
    all_asks = remote(ask.at[everyone], asked.at[everyone], ask_send, ask_recv, next_one)
    all_answers = remote(answer.at[everyone], answered.at[everyone], ans_send, ans_recv, next_one)

    start_halo = [pot_hbm.at[0], pot_hbm.at[n_x - 1]], lines, pot, lines_in, halo_send, halo_recv
    start(halo(*start_halo))

    def send_ask(step, _):
        other = lax.rem(track + step, n_track)
        remote(ask.at[other], asked.at[track], ask_send, ask_recv, (head, other)).start()
        return 0

    lax.fori_loop(1, n_track, send_ask, 0)
    start(rim_copies(n_head, n_track, edge, rim, rim_send, rim_recv, False))
    for copy in large:
        copy.wait()
    for copy in loads[-2:]:
        copy.start()

    edge_rows = 32

    def sweep_chunk(source, target, row, rows_at, unroll, beside=None):
        rows = slice(ROW0 + row, ROW0 + row + rows_at)

        def planes(base, count, carried):
            for j in range(count):
                target[base + j + 1, rows, :], carried = swept(source, src, faces, j, base + j, row, rows_at, carried)
            return carried

        def trip(i, carried):
            if beside is not None:
                beside(i)
            return planes(1 + unroll * i, unroll, carried)

        trips = (n_x - 2) // unroll
        carried = planes(1, unroll, face(source[1, rows, :], source[2, rows, :]))
        carried = lax.fori_loop(1, trips, trip, carried)
        if beside is not None:
            beside(trips)
        planes(1 + unroll * trips, n_x - 2 - unroll * trips, carried)

    def sweep_inner(source, target):
        sweep_chunk(source, target, edge_rows, n_y - 2 * edge_rows, 4)

    def sweep_outer(source, target):
        for side, x in enumerate((0, n_x - 1)):
            for row in range(0, n_y, edge_rows):
                rows = slice(ROW0 + row, ROW0 + row + edge_rows)
                carried = face(source[x, rows, :], source[x + 1, rows, :])
                slot = 4 * side + row // edge_rows
                target[x + 1, rows, :], _ = swept(source, src, faces, slot, x, row, edge_rows, carried)

    def sweep_edge(source, target, row, beside=None):
        sweep_chunk(source, target, row, edge_rows, 8, beside)

    sweep_inner(pot, mid)
    finish(halo_waits(*start_halo), False)
    place_lines(lines_in, pot)
    sweep_outer(pot, mid)
    mid_halo = [mid.at[1, inner, :], mid.at[n_x, inner, :]], lines_mid, mid, lines_mid_in, mid_send, mid_recv
    sends = halo(*mid_halo)
    start(sends[:2])
    sweep_edge(pot, mid, 0)
    lines_mid[0] = mid[1 : n_x + 1, ROW0 : ROW0 + 1, :]
    start(sends[2:3])
    sweep_edge(pot, mid, n_y - edge_rows)
    lines_mid[1] = mid[1 : n_x + 1, ROW0 + n_y - 1 : ROW0 + n_y, :]
    start(sends[3:])

    sweep_inner(mid, pot)
    small[0].wait()
    kernels = []
    for odd in range(2):
        weights = jnp.zeros((8, 128), F32)
        for comp in range(3):
            weights = weights + jnp.where(
                rows8 == 2 * comp + odd, jnp.broadcast_to(dk[comp : comp + 1, :], (8, 128)), 0.0
            )
        high = weights.astype(BF16).astype(F32)
        kernels.append(jnp.concatenate([high, weights - high], axis=0))
    kernels = jnp.concatenate(kernels, axis=0).astype(BF16)
    kernels = jnp.concatenate([kernels, kernels], axis=1)

    def surface(i):
        for j in range(4):
            at = 4 * (i - 1) + j
            both = [halves(pot[2 * at + odd + 1, ROW0 : ROW0 + n_y, :]) for odd in range(2)]
            found = mxu(kernels, jnp.concatenate(both, axis=0), NT)
            total = (found[0:8, :n_y] + found[8:16, :n_y]) + (found[16:24, n_y:] + found[24:32, n_y:])
            surf[pl.ds(8 * at if isinstance(at, int) else pl.multiple_of(8 * at, 8), 8), :] = total

    finish(halo_waits(*mid_halo), False)
    place_lines(lines_mid_in, mid)
    sweep_outer(mid, pot)
    sweep_edge(mid, pot, 0)
    sweep_edge(mid, pot, n_y - edge_rows, surface)
    surface(n_x // 8)

    all_asks.wait_recv()
    table = halves(surf[...])

    def reply(far_y, own):
        y, z, x = track // 8, (track // 4) % 2, track % 4
        others = [
            (y + far_y) % 4 * 8 + (z + far_z) % 2 * 4 + (x + far_x) % 4
            for far_z in (1, 0)
            for far_x in (2, 1, 3, 0)
        ]
        for other in others:
            low, high = lookup(table, [asked[other, 0:1, :], asked[other, 1:2, :]])
            answer[other] = jnp.where(rows8 % 2 == 0, low, pltpu.roll(high, 1, 0))
        if own:
            answered[track] = answer[track]
            others = others[:-1]
        for other in others:
            remote(answer.at[other], answered.at[track], ans_send, ans_recv, (head, other)).start()

    def reply_far(group, _):
        reply(jnp.where(group == 0, 2, jnp.where(group == 1, 1, 3)), False)
        return 0

    lax.fori_loop(0, 3, reply_far, 0)
    reply(0, True)

    def set_lhs(tile, value, comp):
        high = value.astype(BF16).astype(F32)
        lhs[pl.ds(16 * tile + comp, value.shape[0], stride=16), :] = high
        lhs[pl.ds(16 * tile + 8 + comp, value.shape[0], stride=16), :] = value - high

    lhs[...] = jnp.zeros(lhs.shape, F32)
    finish(rim_copies(n_head, n_track, edge, rim, rim_send, rim_recv, True), False)
    for side, tile in ((0, 0), (1, n_tiles + 1)):
        high = rim[side].astype(BF16).astype(F32)
        lhs[16 * tile : 16 * tile + 8, :] = high
        lhs[16 * tile + 8 : 16 * tile + 16, :] = rim[side] - high
    state = [mag[comp] for comp in range(3)]
    for comp in range(3):
        set_lhs(1, state[comp], comp)
    for copy in [*small[1:], *loads[-2:]]:
        copy.wait()

    def first_exchange(k, _):
        self_high, self_low = split(tself[k])
        next_high, next_low = split(tnext[k])
        near_high[k] = jnp.concatenate([self_high, next_high], axis=1)
        near_low[k] = jnp.concatenate([self_low, next_low], axis=1)
        above[k] = jnp.concatenate([next_high, next_low], axis=0)
        exchange(k, lhs, near_high, near_low, above, ex)
        return 0

    def next_exchange(k, _):
        exchange(k, lhs, near_high, near_low, above, ex)
        return 0

    lax.fori_loop(0, n_tiles, first_exchange, 0, unroll=4)
    profile = jnp.broadcast_to(prof[...], (8, 128))
    temp = jnp.concatenate(
        [jnp.take_along_axis(profile, tidx[at : at + 8, :], axis=1) for at in range(0, n_tiles, 8)], axis=0
    )
    target = 0.05 + jnp.maximum(1.0 - temp, 0.0)

    all_answers.wait_recv()
    table = halves(answered[...].reshape(8 * n_track, 128))
    applied = [[None] * n_tiles for _ in range(3)]

    def find(pair):
        found = lookup(table, [addr[2 * pair + i : 2 * pair + i + 1, :] for i in range(2)])
        for i, value in enumerate(found):
            for comp in range(3):
                applied[comp][2 * pair + i] = value[2 * comp : 2 * comp + 1, :]

    last_pair = n_tiles // 2 - 1
    find(0)
    find(last_pair)
    exs = get_ex(ex)
    blank = jnp.zeros((6, width), F32)
    sides = []
    for rows, order in ((slice(0, 8), (0, 1, None)), (slice(n_tiles - 8, n_tiles), (None, n_tiles - 2, n_tiles - 1))):
        fields = [
            jnp.concatenate([blank if at is None else applied[comp][at] for at in order], axis=0) + exs[comp][rows]
            for comp in range(3)
        ]
        sides.append(llb_section([m[rows] for m in state], fields, target[rows]))
    put_edges(edge_new, sides)
    start(rim_copies(n_head, n_track, edge_new, rim_new, rim_new_send, rim_new_recv, False))
    for pair in range(1, last_pair):
        find(pair)
    applied = [jnp.concatenate(rows, axis=0) for rows in applied]
    state = llb_section(state, [a + e for a, e in zip(applied, exs)], target)
    for comp in range(3):
        state_out[comp] = state[comp]
        applied_out[comp] = applied[comp]
    target_out[...] = target

    lhs[0:16, :] = jnp.zeros((16, width), F32)
    lhs[16 * (n_tiles + 1) :, :] = jnp.zeros((16, width), F32)
    for comp in range(3):
        set_lhs(1, state[comp], comp)
    lax.fori_loop(0, EARLY, next_exchange, 0, unroll=4)

    all_asks.wait_send()
    all_answers.wait_send()
    finish(halo_waits(*start_halo), True)
    finish(halo_waits(*mid_halo), True)
    finish(rim_copies(n_head, n_track, edge, rim, rim_send, rim_recv, True), True)
    new_rim = rim_copies(n_head, n_track, edge_new, rim_new, rim_new_send, rim_new_recv, True)
    finish(new_rim, True)
    finish(new_rim, False)


def last_kernel(
    pot, near_high, near_low, above, lhs, ex_early, rim_new, state_in, applied, target,
    relaxed_hbm, magnet_hbm,
    ex, state_out, sem,
):
    n_x, n_y, _ = relaxed_hbm.shape
    n_tiles, width = target.shape
    part = n_x // PARTS
    stores = [
        pltpu.make_async_copy(
            pot.at[pl.ds(part * i + 1, part), pl.ds(ROW0, n_y), :], relaxed_hbm.at[pl.ds(part * i, part), :, :], sem.at[i]
        )
        for i in range(PARTS)
    ]
    for store in stores:
        store.start()
    ex[0 : 8 * EARLY, :] = ex_early[0 : 8 * EARLY, :]

    def next_exchange(k, _):
        exchange(k, lhs, near_high, near_low, above, ex)
        return 0

    lax.fori_loop(EARLY, n_tiles, next_exchange, 0, unroll=4)
    for side, tile in ((0, 0), (1, n_tiles - 1)):
        high = rim_new[side].astype(BF16).astype(F32)
        both = jnp.concatenate([high, rim_new[side] - high], axis=0).astype(BF16)
        if side == 0:
            parts = mxu(both, near_high[tile][:, width:], NT) + mxu(both, near_low[tile][:, width:], NT)
        else:
            parts = mxu(jnp.concatenate([both, both], axis=1), above[tile], NN)
        ex[8 * tile : 8 * tile + 8, :] = ex[8 * tile : 8 * tile + 8, :] + fold(parts)
    state = [state_in[comp] for comp in range(3)]
    fields = [applied[comp] + e for comp, e in enumerate(get_ex(ex))]
    for comp, value in enumerate(llb_section(state, fields, target[...])):
        state_out[comp] = value
    copy = pltpu.make_async_copy(state_out, magnet_hbm, sem.at[PARTS])
    copy.start()
    copy.wait()
    for store in stores:
        store.wait()


def per_device(n_head, n_track, potential, source, depth_kernel, magnet, footprint, temp_index, temp_profile, self_tiles, next_tiles):
    n_x, n_y, n_z = potential.shape
    n_tiles, width = self_tiles.shape[1], self_tiles.shape[2]
    padded = (n_x + 2, n_y + 16, n_z)
    hbm, vmem, dma = pltpu.HBM, pltpu.VMEM, pltpu.SemaphoreType.DMA
    in_hbm = pl.BlockSpec(memory_space=hbm)
    in_vmem = pl.BlockSpec(memory_space=vmem)
    arguments = (
        potential,
        source,
        depth_kernel,
        magnet.reshape(3, n_tiles, width),
        footprint.reshape(n_tiles, width),
        temp_index.reshape(n_tiles, width),
        temp_profile.reshape(1, -1),
        self_tiles[0],
        next_tiles[0],
    )
    arguments = [pltpu.with_memory_space_constraint(a, hbm) for a in arguments]
    grains = (3, n_tiles, width)
    shared = (
        vmem(padded, F32),
        vmem((n_tiles, width, 2 * width), BF16),
        vmem((n_tiles, width, 2 * width), BF16),
        vmem((n_tiles, 2 * width, width), BF16),
        vmem((16 * (n_tiles + 2), width), F32),
        vmem((8 * n_tiles, width), F32),
        vmem((2, 8, width), F32),
        vmem(grains, F32),
        vmem(grains, F32),
        vmem((n_tiles, width), F32),
    )
    results = pl.pallas_call(
        functools.partial(main_kernel, n_head, n_track),
        out_shape=shared,
        in_specs=[in_hbm] * 9,
        out_specs=(in_vmem,) * len(shared),
        scratch_shapes=[
            vmem(padded, F32),
            vmem((n_x, n_y, n_z), F32),
            vmem((2, 8, n_y, n_z), F32),
            vmem((3, n_z), F32),
            vmem(grains, F32),
            vmem((n_tiles, width), I32),
            vmem((n_tiles, width), I32),
            vmem((1, 128), F32),
            vmem((n_tiles, width, width), F32),
            vmem((n_tiles, width, width), F32),
            *[vmem((2, 8, width), F32)] * 3,
            *[vmem((2, n_x, 1, n_z), F32)] * 4,
            vmem((n_tiles, width), I32),
            vmem((n_track, 2, width), I32),
            vmem((n_track, 2, width), I32),
            vmem((8 * (n_x // 2), n_y), F32),
            vmem((n_track, 8, width), F32),
            vmem((n_track, 8, width), F32),
            dma((9 + 2 * PARTS,)),
            *[dma((4,))] * 4,
            *[dma((2,))] * 4,
            *[dma] * 4,
        ],
        compiler_params=pltpu.CompilerParams(
            collective_id=0, has_side_effects=True, vmem_limit_bytes=24 << 20
        ),
        name="pole_and_grains",
    )(*arguments)
    relaxed, magnet_out = pl.pallas_call(
        last_kernel,
        out_shape=(hbm(potential.shape, F32), hbm(grains, F32)),
        in_specs=[in_vmem] * len(shared),
        out_specs=(in_hbm, in_hbm),
        scratch_shapes=[vmem((8 * n_tiles, width), F32), vmem(grains, F32), dma((PARTS + 1,))],
        compiler_params=pltpu.CompilerParams(vmem_limit_bytes=4 << 20),
        name="results",
    )(*results)
    return relaxed, magnet_out.reshape(magnet.shape)


def solution(mesh):
    in_specs = (
        P("head", "track", None),
        P("head", "track", None),
        P(),
        P(None, "track", "head"),
        P("track", "head"),
        P("track", "head"),
        P(),
        P("track", "head", None, None),
        P("track", "head", None, None),
    )
    out_specs = (P("head", "track", None), P(None, "track", "head"))
    return jax.shard_map(
        functools.partial(per_device, mesh.shape["head"], mesh.shape["track"]),
        mesh=mesh,
        in_specs=in_specs,
        out_specs=out_specs,
        check_vma=False,
    )
```

```python
import functools

import jax
import jax.numpy as jnp
from jax import lax
from jax.experimental import pallas as pl
from jax.experimental.pallas import tpu as pltpu
from jax.sharding import PartitionSpec as P

F32 = jnp.float32
BF16 = jnp.bfloat16
I32 = jnp.int32
NN = (((1,), (0,)), ((), ()))
NT = (((1,), (1,)), ((), ()))
ROW0 = 8
PARTS = 4
EARLY = 24


def mxu(a, b, dims):
    return lax.dot_general(a, b, dims, preferred_element_type=F32)


def split(a):
    high = a.astype(BF16)
    return high, (a - high.astype(F32)).astype(BF16)


def face(a, b):
    differ = b - a
    perm = 1.0 + pltpu.reciprocal(0.25 + differ * differ)
    return perm, perm * differ


def one_hot_rows(index, count):
    lanes = index.shape[1]
    rows = lax.broadcasted_iota(I32, (count, lanes), 0)
    return jnp.where(rows == jnp.broadcast_to(index, (count, lanes)), 1.0, 0.0)


def lookup(table, address):
    hot = jnp.concatenate([one_hot_rows(a & 127, 128) for a in address], axis=1).astype(BF16)
    found = mxu(table, jnp.concatenate([hot, hot], axis=0), NN)
    results = []
    for part, a in enumerate(address):
        group = jnp.broadcast_to(a >> 8, (8, 128))
        odd = jnp.broadcast_to((a >> 7) & 1, (8, 128))
        total = jnp.zeros((8, 128), F32)
        for g in range(table.shape[0] // 8):
            total = total + jnp.where(
                group == g, found[8 * g : 8 * g + 8, 128 * part : 128 * part + 128], 0.0
            )
        results.append(jnp.where(odd == 0, total, pltpu.roll(total, 7, 0)))
    return results


def halves(rows):
    high, low = split(rows)
    return jnp.concatenate([high, low], axis=1)


def llb_section(state, field, target):
    mx, my, mz = state
    sq_norm = mx * mx + my * my + mz * mz
    pull = 0.5 * (1.0 - sq_norm / target)
    hx, hy, hz = (f + pull * m for f, m in zip(field, state))
    tx, ty, tz = my * hz - mz * hy, mz * hx - mx * hz, mx * hy - my * hx
    dx, dy, dz = my * tz - mz * ty, mz * tx - mx * tz, mx * ty - my * tx
    along = 0.3 * (mx * hx + my * hy + mz * hz)
    return tuple(
        m + 0.1 * (along * m - t - 0.5 * d)
        for m, t, d in zip(state, (tx, ty, tz), (dx, dy, dz))
    )


def has_neighbours(n_head, n_track):
    head = lax.axis_index("head")
    track = lax.axis_index("track")
    return head, track, head > 0, head < n_head - 1, track > 0, track < n_track - 1


def remote(a, b, send, recv, device):
    return pltpu.make_async_remote_copy(
        src_ref=a, dst_ref=b, send_sem=send, recv_sem=recv, device_id=device,
        device_id_type=pl.DeviceIdType.MESH,
    )


def start(copies):
    for there, copy in copies:

        @pl.when(there)
        def _():
            copy.start()


def finish(copies, sent):
    for there, copy in copies:

        @pl.when(there)
        def _():
            if sent:
                copy.wait_send()
            else:
                copy.wait_recv()


def greet(n_head, n_track):
    head, track, has_low_x, has_high_x, _, _ = has_neighbours(n_head, n_track)
    barrier = pltpu.get_barrier_semaphore()

    def hello(step, _):
        other = (head, lax.rem(track + step, n_track))
        pl.semaphore_signal(barrier, inc=1, device_id=other, device_id_type=pl.DeviceIdType.MESH)
        return 0

    lax.fori_loop(1, n_track, hello, 0)
    for there, other in ((has_low_x, head - 1), (has_high_x, head + 1)):

        @pl.when(there)
        def _():
            pl.semaphore_signal(
                barrier, inc=1, device_id=(other, track), device_id_type=pl.DeviceIdType.MESH
            )

    return barrier, n_track - 1 + has_low_x.astype(I32) + has_high_x.astype(I32)


def rim_copies(n_head, n_track, source, target, send, recv, waits):
    head, track, has_low_x, has_high_x, _, _ = has_neighbours(n_head, n_track)
    low, high = (head - 1, track), (head + 1, track)
    if waits:
        return [
            (has_low_x, remote(source.at[0], target.at[0], send.at[0], recv.at[0], low)),
            (has_high_x, remote(source.at[1], target.at[1], send.at[1], recv.at[1], high)),
        ]
    return [
        (has_low_x, remote(source.at[0], target.at[1], send.at[0], recv.at[1], low)),
        (has_high_x, remote(source.at[1], target.at[0], send.at[1], recv.at[0], high)),
    ]


def put_edges(edge, sides):
    edge[...] = jnp.zeros(edge.shape, F32)
    for comp in range(3):
        low, high = sides[0][comp], sides[1][comp]
        last = high.shape[0] - 1
        edge[0, comp : comp + 1, :] = low[0:1, :]
        edge[1, comp : comp + 1, :] = high[last : last + 1, :]


def rank_grains(foot, addr, ask, n_track):
    later = lax.broadcasted_iota(I32, (128, 128), 0) < lax.broadcasted_iota(I32, (128, 128), 1)
    count_matrix = jnp.concatenate(
        [jnp.where(later, 1.0, 0.0), jnp.ones((128, 128), F32)], axis=1
    ).astype(BF16)
    before = jnp.zeros((n_track, 128), F32)
    asks = jnp.zeros((128, 128), F32)
    for chunk in range(foot.shape[0]):
        cell = foot[chunk : chunk + 1, :]
        owner = cell >> 13
        hot = one_hot_rows(owner, n_track)
        counts = mxu(hot.astype(BF16), count_matrix, NN)
        place = jnp.sum(hot * (counts[:, :128] + before), axis=0, keepdims=True).astype(I32)
        before = before + counts[:, 128:]
        where_at = owner * 256 + place
        addr[chunk : chunk + 1, :] = where_at
        row = one_hot_rows(where_at >> 7, 2 * n_track)
        lane = one_hot_rows(where_at & 127, 128)
        high = jnp.broadcast_to((cell >> 7) & 63, row.shape).astype(F32)
        low = jnp.broadcast_to(cell & 127, row.shape).astype(F32)
        values = jnp.concatenate([row * high, row * low], axis=0)
        asks = asks + mxu(values.astype(BF16), lane.astype(BF16), NT)
    cells = (asks[: 2 * n_track] * 128.0 + asks[2 * n_track :]).astype(I32)
    for owner in range(n_track):
        ask[owner, 0:2, :] = cells[2 * owner : 2 * owner + 2, :]


def swept(source, src, faces, slot, x, row, rows_at, carried):
    lanes = lax.broadcasted_iota(I32, (rows_at, 128), 1)
    o = ROW0 + row
    center = source[x + 1, o : o + rows_at, :]
    depth = center.shape[1]
    perm, flux = face(center, source[x + 2, o : o + rows_at, :])
    numer = (src[x, row : row + rows_at, :] - carried[1]) + flux
    denom = (1.0 + carried[0]) + perm
    carried = (perm, flux)
    perm, flux = face(source[x + 1, o - 1 : o - 1 + rows_at, :], center)
    faces[0, slot, 0:rows_at, :] = perm
    faces[1, slot, 0:rows_at, :] = flux
    numer = numer - flux
    denom = denom + perm
    end = o + rows_at
    perm, flux = face(source[x + 1, end - 1 : end, :], source[x + 1, end : end + 1, :])
    faces[0, slot, rows_at : rows_at + 1, :] = perm
    faces[1, slot, rows_at : rows_at + 1, :] = flux
    for other in (
        jnp.where(lanes == depth - 1, 0.0, pltpu.roll(center, depth - 1, 1)),
        jnp.where(lanes == 0, 0.0, pltpu.roll(center, 1, 1)),
    ):
        perm, flux = face(center, other)
        numer = numer + flux
        denom = denom + perm
    numer = numer + faces[1, slot, 1 : rows_at + 1, :]
    denom = denom + faces[0, slot, 1 : rows_at + 1, :]
    return center + (0.8 * numer) * pltpu.reciprocal(denom), carried


def fold(parts):
    return parts[:8] + parts[8:]


def exchange(k, lhs, near_high, near_low, above, ex):
    def get_lhs(tile):
        return lhs[pl.ds(pl.multiple_of(16 * tile, 16), 16), :].astype(BF16)

    near = jnp.concatenate([get_lhs(k + 1), get_lhs(k)], axis=1)
    far = get_lhs(k + 2)
    parts = mxu(near, near_high[k], NT) + mxu(near, near_low[k], NT)
    parts = parts + mxu(jnp.concatenate([far, far], axis=1), above[k], NN)
    ex[pl.ds(pl.multiple_of(8 * k, 8), 8), :] = fold(parts)


def get_ex(ex):
    return [ex[pl.ds(comp, ex.shape[0] // 8, stride=8), :] for comp in range(3)]


def main_kernel(
    n_head, n_track,
    pot_hbm, src_hbm, dk_hbm, mag_hbm, foot_hbm, temp_hbm, prof_hbm, self_hbm, next_hbm,
    pot, near_high, near_low, above, lhs, ex, rim_new, state_out, applied_out, target_out,
    mid, src, faces, dk, mag, foot, tidx, prof, tself, tnext,
    rim, edge, edge_new, lines, lines_in, lines_mid, lines_mid_in,
    addr, ask, asked, surf, answer, answered,
    in_sem, halo_send, halo_recv, mid_send, mid_recv, rim_send, rim_recv,
    rim_new_send, rim_new_recv, ask_send, ask_recv, ans_send, ans_recv,
):
    head, track, has_low_x, has_high_x, has_low_y, has_high_y = has_neighbours(n_head, n_track)
    n_x, n_y, n_z = src.shape
    n_tiles, width = mag.shape[1:]
    inner, all_x = pl.ds(ROW0, n_y), pl.ds(1, n_x)
    low_x, high_x = (head - 1, track), (head + 1, track)
    low_y, high_y = (head, track - 1), (head, track + 1)
    rows8 = lax.broadcasted_iota(I32, (8, 128), 0)

    barrier, n_greeted = greet(n_head, n_track)
    part = n_x // PARTS
    parts = range(0, n_x, part)
    pairs = [
        (foot_hbm, foot),
        (mag_hbm, mag),
        (pot_hbm.at[:, pl.ds(0, 1), :], lines.at[0]),
        (pot_hbm.at[:, pl.ds(n_y - 1, 1), :], lines.at[1]),
        *[(pot_hbm.at[pl.ds(x, part), :, :], pot.at[pl.ds(x + 1, part), inner, :]) for x in parts],
        *[(src_hbm.at[pl.ds(x, part), :, :], src.at[pl.ds(x, part), :, :]) for x in parts],
        (dk_hbm, dk),
        (temp_hbm, tidx),
        (prof_hbm, prof),
        (self_hbm, tself),
        (next_hbm, tnext),
    ]
    loads = [pltpu.make_async_copy(a, b, in_sem.at[i]) for i, (a, b) in enumerate(pairs)]
    large = loads[4 : 4 + 2 * PARTS]
    small = loads[4 + 2 * PARTS : -2]
    for copy in loads[:-2]:
        copy.start()

    for side, there in enumerate((has_low_x, has_high_x)):

        @pl.when(jnp.logical_not(there))
        def _():
            for ref in (pot, mid):
                ref[side * (n_x + 1), ROW0 : ROW0 + n_y, :] = jnp.zeros((n_y, n_z), F32)
            for ref in (rim, rim_new):
                ref[side] = jnp.zeros(ref.shape[1:], F32)

    for side, there in enumerate((has_low_y, has_high_y)):

        @pl.when(jnp.logical_not(there))
        def _():
            for ref in (lines_in, lines_mid_in):
                ref[side] = jnp.zeros(ref.shape[1:], F32)

    loads[0].wait()
    rank_grains(foot, addr, ask, n_track)
    asked[track] = ask[track]
    loads[1].wait()
    put_edges(edge, [[mag[comp] for comp in range(3)]] * 2)
    loads[2].wait()
    loads[3].wait()
    pl.semaphore_wait(barrier, n_greeted)

    def halo(planes, rows, target, rows_in, send, recv):
        return [
            (has_low_x, remote(planes[0], target.at[n_x + 1, inner, :], send.at[0], recv.at[1], low_x)),
            (has_high_x, remote(planes[1], target.at[0, inner, :], send.at[1], recv.at[0], high_x)),
            (has_low_y, remote(rows.at[0], rows_in.at[1], send.at[2], recv.at[3], low_y)),
            (has_high_y, remote(rows.at[1], rows_in.at[0], send.at[3], recv.at[2], high_y)),
        ]

    def halo_waits(planes, rows, target, rows_in, send, recv):
        return [
            (has_low_x, remote(planes[0], target.at[0, inner, :], send.at[0], recv.at[0], low_x)),
            (has_high_x, remote(planes[1], target.at[n_x + 1, inner, :], send.at[1], recv.at[1], high_x)),
            (has_low_y, remote(rows.at[0], rows_in.at[0], send.at[2], recv.at[2], low_y)),
            (has_high_y, remote(rows.at[1], rows_in.at[1], send.at[3], recv.at[3], high_y)),
        ]

    def place_lines(rows_in, target):
        target[1 : n_x + 1, ROW0 - 1 : ROW0, :] = rows_in[0]
        target[1 : n_x + 1, ROW0 + n_y : ROW0 + n_y + 1, :] = rows_in[1]

    everyone = pl.ds(0, n_track - 1)
    next_one = (head, lax.rem(track + 1, n_track))
    all_asks = remote(ask.at[everyone], asked.at[everyone], ask_send, ask_recv, next_one)
    all_answers = remote(answer.at[everyone], answered.at[everyone], ans_send, ans_recv, next_one)

    start_halo = [pot_hbm.at[0], pot_hbm.at[n_x - 1]], lines, pot, lines_in, halo_send, halo_recv
    start(halo(*start_halo))

    def send_ask(step, _):
        other = lax.rem(track + step, n_track)
        remote(ask.at[other], asked.at[track], ask_send, ask_recv, (head, other)).start()
        return 0

    lax.fori_loop(1, n_track, send_ask, 0)
    start(rim_copies(n_head, n_track, edge, rim, rim_send, rim_recv, False))
    for copy in large:
        copy.wait()
    for copy in loads[-2:]:
        copy.start()

    edge_rows = 32

    def sweep_chunk(source, target, row, rows_at, unroll, beside=None):
        rows = slice(ROW0 + row, ROW0 + row + rows_at)

        def planes(base, count, carried):
            for j in range(count):
                target[base + j + 1, rows, :], carried = swept(source, src, faces, j, base + j, row, rows_at, carried)
            return carried

        def trip(i, carried):
            if beside is not None:
                beside(i)
            return planes(1 + unroll * i, unroll, carried)

        trips = (n_x - 2) // unroll
        carried = planes(1, unroll, face(source[1, rows, :], source[2, rows, :]))
        carried = lax.fori_loop(1, trips, trip, carried)
        if beside is not None:
            beside(trips)
        planes(1 + unroll * trips, n_x - 2 - unroll * trips, carried)

    def sweep_inner(source, target):
        sweep_chunk(source, target, edge_rows, n_y - 2 * edge_rows, 8)

    def sweep_outer(source, target):
        for side, x in enumerate((0, n_x - 1)):
            for row in range(0, n_y, edge_rows):
                rows = slice(ROW0 + row, ROW0 + row + edge_rows)
                carried = face(source[x, rows, :], source[x + 1, rows, :])
                slot = 4 * side + row // edge_rows
                target[x + 1, rows, :], _ = swept(source, src, faces, slot, x, row, edge_rows, carried)

    def sweep_edge(source, target, row, beside=None):
        sweep_chunk(source, target, row, edge_rows, 8, beside)

    sweep_inner(pot, mid)
    finish(halo_waits(*start_halo), False)
    place_lines(lines_in, pot)
    sweep_outer(pot, mid)
    mid_halo = [mid.at[1, inner, :], mid.at[n_x, inner, :]], lines_mid, mid, lines_mid_in, mid_send, mid_recv
    sends = halo(*mid_halo)
    start(sends[:2])
    sweep_edge(pot, mid, 0)
    lines_mid[0] = mid[1 : n_x + 1, ROW0 : ROW0 + 1, :]
    start(sends[2:3])
    sweep_edge(pot, mid, n_y - edge_rows)
    lines_mid[1] = mid[1 : n_x + 1, ROW0 + n_y - 1 : ROW0 + n_y, :]
    start(sends[3:])

    sweep_inner(mid, pot)
    small[0].wait()
    kernels = []
    for odd in range(2):
        weights = jnp.zeros((8, 128), F32)
        for comp in range(3):
            weights = weights + jnp.where(
                rows8 == 2 * comp + odd, jnp.broadcast_to(dk[comp : comp + 1, :], (8, 128)), 0.0
            )
        high = weights.astype(BF16).astype(F32)
        kernels.append(jnp.concatenate([high, weights - high], axis=0))
    kernels = jnp.concatenate(kernels, axis=0).astype(BF16)
    kernels = jnp.concatenate([kernels, kernels], axis=1)

    def surface(i):
        for j in range(4):
            at = 4 * (i - 1) + j
            both = [halves(pot[2 * at + odd + 1, ROW0 : ROW0 + n_y, :]) for odd in range(2)]
            found = mxu(kernels, jnp.concatenate(both, axis=0), NT)
            total = (found[0:8, :n_y] + found[8:16, :n_y]) + (found[16:24, n_y:] + found[24:32, n_y:])
            surf[pl.ds(8 * at if isinstance(at, int) else pl.multiple_of(8 * at, 8), 8), :] = total

    finish(halo_waits(*mid_halo), False)
    place_lines(lines_mid_in, mid)
    sweep_outer(mid, pot)
    sweep_edge(mid, pot, 0)
    sweep_edge(mid, pot, n_y - edge_rows, surface)
    surface(n_x // 8)

    all_asks.wait_recv()
    table = halves(surf[...])

    def reply(far_y, own):
        y, z, x = track // 8, (track // 4) % 2, track % 4
        others = [
            (y + far_y) % 4 * 8 + (z + far_z) % 2 * 4 + (x + far_x) % 4
            for far_z in (1, 0)
            for far_x in (2, 1, 3, 0)
        ]
        for other in others:
            low, high = lookup(table, [asked[other, 0:1, :], asked[other, 1:2, :]])
            answer[other] = jnp.where(rows8 % 2 == 0, low, pltpu.roll(high, 1, 0))
        if own:
            answered[track] = answer[track]
            others = others[:-1]
        for other in others:
            remote(answer.at[other], answered.at[track], ans_send, ans_recv, (head, other)).start()

    def reply_far(group, _):
        reply(jnp.where(group == 0, 2, jnp.where(group == 1, 1, 3)), False)
        return 0

    lax.fori_loop(0, 3, reply_far, 0)
    reply(0, True)

    def set_lhs(tile, value, comp):
        high = value.astype(BF16).astype(F32)
        lhs[pl.ds(16 * tile + comp, value.shape[0], stride=16), :] = high
        lhs[pl.ds(16 * tile + 8 + comp, value.shape[0], stride=16), :] = value - high

    lhs[...] = jnp.zeros(lhs.shape, F32)
    finish(rim_copies(n_head, n_track, edge, rim, rim_send, rim_recv, True), False)
    for side, tile in ((0, 0), (1, n_tiles + 1)):
        high = rim[side].astype(BF16).astype(F32)
        lhs[16 * tile : 16 * tile + 8, :] = high
        lhs[16 * tile + 8 : 16 * tile + 16, :] = rim[side] - high
    state = [mag[comp] for comp in range(3)]
    for comp in range(3):
        set_lhs(1, state[comp], comp)
    for copy in [*small[1:], *loads[-2:]]:
        copy.wait()

    def first_exchange(k, _):
        self_high, self_low = split(tself[k])
        next_high, next_low = split(tnext[k])
        near_high[k] = jnp.concatenate([self_high, next_high], axis=1)
        near_low[k] = jnp.concatenate([self_low, next_low], axis=1)
        above[k] = jnp.concatenate([next_high, next_low], axis=0)
        exchange(k, lhs, near_high, near_low, above, ex)
        return 0

    def next_exchange(k, _):
        exchange(k, lhs, near_high, near_low, above, ex)
        return 0

    lax.fori_loop(0, n_tiles, first_exchange, 0, unroll=4)
    profile = jnp.broadcast_to(prof[...], (8, 128))
    temp = jnp.concatenate(
        [jnp.take_along_axis(profile, tidx[at : at + 8, :], axis=1) for at in range(0, n_tiles, 8)], axis=0
    )
    target = 0.05 + jnp.maximum(1.0 - temp, 0.0)

    all_answers.wait_recv()
    table = halves(answered[...].reshape(8 * n_track, 128))
    applied = [[None] * n_tiles for _ in range(3)]

    def find(pair):
        found = lookup(table, [addr[2 * pair + i : 2 * pair + i + 1, :] for i in range(2)])
        for i, value in enumerate(found):
            for comp in range(3):
                applied[comp][2 * pair + i] = value[2 * comp : 2 * comp + 1, :]

    last_pair = n_tiles // 2 - 1
    find(0)
    find(last_pair)
    exs = get_ex(ex)
    blank = jnp.zeros((6, width), F32)
    sides = []
    for rows, order in ((slice(0, 8), (0, 1, None)), (slice(n_tiles - 8, n_tiles), (None, n_tiles - 2, n_tiles - 1))):
        fields = [
            jnp.concatenate([blank if at is None else applied[comp][at] for at in order], axis=0) + exs[comp][rows]
            for comp in range(3)
        ]
        sides.append(llb_section([m[rows] for m in state], fields, target[rows]))
    put_edges(edge_new, sides)
    start(rim_copies(n_head, n_track, edge_new, rim_new, rim_new_send, rim_new_recv, False))
    for pair in range(1, last_pair):
        find(pair)
    applied = [jnp.concatenate(rows, axis=0) for rows in applied]
    state = llb_section(state, [a + e for a, e in zip(applied, exs)], target)
    for comp in range(3):
        state_out[comp] = state[comp]
        applied_out[comp] = applied[comp]
    target_out[...] = target

    lhs[0:16, :] = jnp.zeros((16, width), F32)
    lhs[16 * (n_tiles + 1) :, :] = jnp.zeros((16, width), F32)
    for comp in range(3):
        set_lhs(1, state[comp], comp)
    lax.fori_loop(0, EARLY, next_exchange, 0, unroll=4)

    all_asks.wait_send()
    all_answers.wait_send()
    finish(halo_waits(*start_halo), True)
    finish(halo_waits(*mid_halo), True)
    finish(rim_copies(n_head, n_track, edge, rim, rim_send, rim_recv, True), True)
    new_rim = rim_copies(n_head, n_track, edge_new, rim_new, rim_new_send, rim_new_recv, True)
    finish(new_rim, True)
    finish(new_rim, False)


def last_kernel(
    pot, near_high, near_low, above, lhs, ex_early, rim_new, state_in, applied, target,
    relaxed_hbm, magnet_hbm,
    ex, state_out, sem,
):
    n_x, n_y, _ = relaxed_hbm.shape
    n_tiles, width = target.shape
    part = n_x // PARTS
    stores = [
        pltpu.make_async_copy(
            pot.at[pl.ds(part * i + 1, part), pl.ds(ROW0, n_y), :], relaxed_hbm.at[pl.ds(part * i, part), :, :], sem.at[i]
        )
        for i in range(PARTS)
    ]
    for store in stores:
        store.start()
    ex[0 : 8 * EARLY, :] = ex_early[0 : 8 * EARLY, :]

    def next_exchange(k, _):
        exchange(k, lhs, near_high, near_low, above, ex)
        return 0

    lax.fori_loop(EARLY, n_tiles, next_exchange, 0, unroll=4)
    for side, tile in ((0, 0), (1, n_tiles - 1)):
        high = rim_new[side].astype(BF16).astype(F32)
        both = jnp.concatenate([high, rim_new[side] - high], axis=0).astype(BF16)
        if side == 0:
            parts = mxu(both, near_high[tile][:, width:], NT) + mxu(both, near_low[tile][:, width:], NT)
        else:
            parts = mxu(jnp.concatenate([both, both], axis=1), above[tile], NN)
        ex[8 * tile : 8 * tile + 8, :] = ex[8 * tile : 8 * tile + 8, :] + fold(parts)
    state = [state_in[comp] for comp in range(3)]
    fields = [applied[comp] + e for comp, e in enumerate(get_ex(ex))]
    for comp, value in enumerate(llb_section(state, fields, target[...])):
        state_out[comp] = value
    copy = pltpu.make_async_copy(state_out, magnet_hbm, sem.at[PARTS])
    copy.start()
    copy.wait()
    for store in stores:
        store.wait()


def per_device(n_head, n_track, potential, source, depth_kernel, magnet, footprint, temp_index, temp_profile, self_tiles, next_tiles):
    n_x, n_y, n_z = potential.shape
    n_tiles, width = self_tiles.shape[1], self_tiles.shape[2]
    padded = (n_x + 2, n_y + 16, n_z)
    hbm, vmem, dma = pltpu.HBM, pltpu.VMEM, pltpu.SemaphoreType.DMA
    in_hbm = pl.BlockSpec(memory_space=hbm)
    in_vmem = pl.BlockSpec(memory_space=vmem)
    arguments = (
        potential,
        source,
        depth_kernel,
        magnet.reshape(3, n_tiles, width),
        footprint.reshape(n_tiles, width),
        temp_index.reshape(n_tiles, width),
        temp_profile.reshape(1, -1),
        self_tiles[0],
        next_tiles[0],
    )
    arguments = [pltpu.with_memory_space_constraint(a, hbm) for a in arguments]
    grains = (3, n_tiles, width)
    shared = (
        vmem(padded, F32),
        vmem((n_tiles, width, 2 * width), BF16),
        vmem((n_tiles, width, 2 * width), BF16),
        vmem((n_tiles, 2 * width, width), BF16),
        vmem((16 * (n_tiles + 2), width), F32),
        vmem((8 * n_tiles, width), F32),
        vmem((2, 8, width), F32),
        vmem(grains, F32),
        vmem(grains, F32),
        vmem((n_tiles, width), F32),
    )
    results = pl.pallas_call(
        functools.partial(main_kernel, n_head, n_track),
        out_shape=shared,
        in_specs=[in_hbm] * 9,
        out_specs=(in_vmem,) * len(shared),
        scratch_shapes=[
            vmem(padded, F32),
            vmem((n_x, n_y, n_z), F32),
            vmem((2, 8, n_y, n_z), F32),
            vmem((3, n_z), F32),
            vmem(grains, F32),
            vmem((n_tiles, width), I32),
            vmem((n_tiles, width), I32),
            vmem((1, 128), F32),
            vmem((n_tiles, width, width), F32),
            vmem((n_tiles, width, width), F32),
            *[vmem((2, 8, width), F32)] * 3,
            *[vmem((2, n_x, 1, n_z), F32)] * 4,
            vmem((n_tiles, width), I32),
            vmem((n_track, 2, width), I32),
            vmem((n_track, 2, width), I32),
            vmem((8 * (n_x // 2), n_y), F32),
            vmem((n_track, 8, width), F32),
            vmem((n_track, 8, width), F32),
            dma((9 + 2 * PARTS,)),
            *[dma((4,))] * 4,
            *[dma((2,))] * 4,
            *[dma] * 4,
        ],
        compiler_params=pltpu.CompilerParams(
            collective_id=0, has_side_effects=True, vmem_limit_bytes=24 << 20
        ),
        name="pole_and_grains",
    )(*arguments)
    relaxed, magnet_out = pl.pallas_call(
        last_kernel,
        out_shape=(hbm(potential.shape, F32), hbm(grains, F32)),
        in_specs=[in_vmem] * len(shared),
        out_specs=(in_hbm, in_hbm),
        scratch_shapes=[vmem((8 * n_tiles, width), F32), vmem(grains, F32), dma((PARTS + 1,))],
        compiler_params=pltpu.CompilerParams(vmem_limit_bytes=4 << 20),
        name="results",
    )(*results)
    return relaxed, magnet_out.reshape(magnet.shape)


def solution(mesh):
    in_specs = (
        P("head", "track", None),
        P("head", "track", None),
        P(),
        P(None, "track", "head"),
        P("track", "head"),
        P("track", "head"),
        P(),
        P("track", "head", None, None),
        P("track", "head", None, None),
    )
    out_specs = (P("head", "track", None), P(None, "track", "head"))
    return jax.shard_map(
        functools.partial(per_device, mesh.shape["head"], mesh.shape["track"]),
        mesh=mesh,
        in_specs=in_specs,
        out_specs=out_specs,
        check_vma=False,
    )
```

```python
import functools

import jax
import jax.numpy as jnp
from jax import lax
from jax.experimental import pallas as pl
from jax.experimental.pallas import tpu as pltpu
from jax.sharding import PartitionSpec as P

F32 = jnp.float32
BF16 = jnp.bfloat16
I32 = jnp.int32
NN = (((1,), (0,)), ((), ()))
NT = (((1,), (1,)), ((), ()))
ROW0 = 8
PARTS = 4
EARLY = 24


def mxu(a, b, dims):
    return lax.dot_general(a, b, dims, preferred_element_type=F32)


def split(a):
    high = a.astype(BF16)
    return high, (a - high.astype(F32)).astype(BF16)


def face(a, b):
    differ = b - a
    perm = 1.0 + pltpu.reciprocal(0.25 + differ * differ)
    return perm, perm * differ


def one_hot_rows(index, count):
    lanes = index.shape[1]
    rows = lax.broadcasted_iota(I32, (count, lanes), 0)
    return jnp.where(rows == jnp.broadcast_to(index, (count, lanes)), 1.0, 0.0)


def lookup(table, address):
    hot = jnp.concatenate([one_hot_rows(a & 127, 128) for a in address], axis=1).astype(BF16)
    found = mxu(table, jnp.concatenate([hot, hot], axis=0), NN)
    results = []
    for part, a in enumerate(address):
        group = jnp.broadcast_to(a >> 8, (8, 128))
        odd = jnp.broadcast_to((a >> 7) & 1, (8, 128))
        total = jnp.zeros((8, 128), F32)
        for g in range(table.shape[0] // 8):
            total = total + jnp.where(
                group == g, found[8 * g : 8 * g + 8, 128 * part : 128 * part + 128], 0.0
            )
        results.append(jnp.where(odd == 0, total, pltpu.roll(total, 7, 0)))
    return results


def halves(rows):
    high, low = split(rows)
    return jnp.concatenate([high, low], axis=1)


def llb_section(state, field, target):
    mx, my, mz = state
    sq_norm = mx * mx + my * my + mz * mz
    pull = 0.5 * (1.0 - sq_norm / target)
    hx, hy, hz = (f + pull * m for f, m in zip(field, state))
    tx, ty, tz = my * hz - mz * hy, mz * hx - mx * hz, mx * hy - my * hx
    dx, dy, dz = my * tz - mz * ty, mz * tx - mx * tz, mx * ty - my * tx
    along = 0.3 * (mx * hx + my * hy + mz * hz)
    return tuple(
        m + 0.1 * (along * m - t - 0.5 * d)
        for m, t, d in zip(state, (tx, ty, tz), (dx, dy, dz))
    )


def has_neighbours(n_head, n_track):
    head = lax.axis_index("head")
    track = lax.axis_index("track")
    return head, track, head > 0, head < n_head - 1, track > 0, track < n_track - 1


def remote(a, b, send, recv, device):
    return pltpu.make_async_remote_copy(
        src_ref=a, dst_ref=b, send_sem=send, recv_sem=recv, device_id=device,
        device_id_type=pl.DeviceIdType.MESH,
    )


def start(copies):
    for there, copy in copies:

        @pl.when(there)
        def _():
            copy.start()


def finish(copies, sent):
    for there, copy in copies:

        @pl.when(there)
        def _():
            if sent:
                copy.wait_send()
            else:
                copy.wait_recv()


def greet(n_head, n_track):
    head, track, has_low_x, has_high_x, _, _ = has_neighbours(n_head, n_track)
    barrier = pltpu.get_barrier_semaphore()

    def hello(step, _):
        other = (head, lax.rem(track + step, n_track))
        pl.semaphore_signal(barrier, inc=1, device_id=other, device_id_type=pl.DeviceIdType.MESH)
        return 0

    lax.fori_loop(1, n_track, hello, 0)
    for there, other in ((has_low_x, head - 1), (has_high_x, head + 1)):

        @pl.when(there)
        def _():
            pl.semaphore_signal(
                barrier, inc=1, device_id=(other, track), device_id_type=pl.DeviceIdType.MESH
            )

    return barrier, n_track - 1 + has_low_x.astype(I32) + has_high_x.astype(I32)


def rim_copies(n_head, n_track, source, target, send, recv, waits):
    head, track, has_low_x, has_high_x, _, _ = has_neighbours(n_head, n_track)
    low, high = (head - 1, track), (head + 1, track)
    if waits:
        return [
            (has_low_x, remote(source.at[0], target.at[0], send.at[0], recv.at[0], low)),
            (has_high_x, remote(source.at[1], target.at[1], send.at[1], recv.at[1], high)),
        ]
    return [
        (has_low_x, remote(source.at[0], target.at[1], send.at[0], recv.at[1], low)),
        (has_high_x, remote(source.at[1], target.at[0], send.at[1], recv.at[0], high)),
    ]


def put_edges(edge, sides):
    edge[...] = jnp.zeros(edge.shape, F32)
    for comp in range(3):
        low, high = sides[0][comp], sides[1][comp]
        last = high.shape[0] - 1
        edge[0, comp : comp + 1, :] = low[0:1, :]
        edge[1, comp : comp + 1, :] = high[last : last + 1, :]


def rank_grains(foot, addr, ask, n_track):
    later = lax.broadcasted_iota(I32, (128, 128), 0) < lax.broadcasted_iota(I32, (128, 128), 1)
    count_matrix = jnp.concatenate(
        [jnp.where(later, 1.0, 0.0), jnp.ones((128, 128), F32)], axis=1
    ).astype(BF16)
    before = jnp.zeros((n_track, 128), F32)
    asks = jnp.zeros((128, 128), F32)
    for chunk in range(foot.shape[0]):
        cell = foot[chunk : chunk + 1, :]
        owner = cell >> 13
        hot = one_hot_rows(owner, n_track)
        counts = mxu(hot.astype(BF16), count_matrix, NN)
        place = jnp.sum(hot * (counts[:, :128] + before), axis=0, keepdims=True).astype(I32)
        before = before + counts[:, 128:]
        where_at = owner * 256 + place
        addr[chunk : chunk + 1, :] = where_at
        row = one_hot_rows(where_at >> 7, 2 * n_track)
        lane = one_hot_rows(where_at & 127, 128)
        high = jnp.broadcast_to((cell >> 7) & 63, row.shape).astype(F32)
        low = jnp.broadcast_to(cell & 127, row.shape).astype(F32)
        values = jnp.concatenate([row * high, row * low], axis=0)
        asks = asks + mxu(values.astype(BF16), lane.astype(BF16), NT)
    cells = (asks[: 2 * n_track] * 128.0 + asks[2 * n_track :]).astype(I32)
    for owner in range(n_track):
        ask[owner, 0:2, :] = cells[2 * owner : 2 * owner + 2, :]


def swept(source, src, faces, slot, x, row, rows_at, carried):
    lanes = lax.broadcasted_iota(I32, (rows_at, 128), 1)
    o = ROW0 + row
    center = source[x + 1, o : o + rows_at, :]
    depth = center.shape[1]
    perm, flux = face(center, source[x + 2, o : o + rows_at, :])
    numer = (src[x, row : row + rows_at, :] - carried[1]) + flux
    denom = (1.0 + carried[0]) + perm
    carried = (perm, flux)
    perm, flux = face(source[x + 1, o - 1 : o - 1 + rows_at, :], center)
    faces[0, slot, 0:rows_at, :] = perm
    faces[1, slot, 0:rows_at, :] = flux
    numer = numer - flux
    denom = denom + perm
    end = o + rows_at
    perm, flux = face(source[x + 1, end - 1 : end, :], source[x + 1, end : end + 1, :])
    faces[0, slot, rows_at : rows_at + 1, :] = perm
    faces[1, slot, rows_at : rows_at + 1, :] = flux
    for other in (
        jnp.where(lanes == depth - 1, 0.0, pltpu.roll(center, depth - 1, 1)),
        jnp.where(lanes == 0, 0.0, pltpu.roll(center, 1, 1)),
    ):
        perm, flux = face(center, other)
        numer = numer + flux
        denom = denom + perm
    numer = numer + faces[1, slot, 1 : rows_at + 1, :]
    denom = denom + faces[0, slot, 1 : rows_at + 1, :]
    return center + (0.8 * numer) * pltpu.reciprocal(denom), carried


def fold(parts):
    return parts[:8] + parts[8:]


def exchange(k, lhs, near_high, near_low, above, ex):
    def get_lhs(tile):
        return lhs[pl.ds(pl.multiple_of(16 * tile, 16), 16), :].astype(BF16)

    near = jnp.concatenate([get_lhs(k + 1), get_lhs(k)], axis=1)
    far = get_lhs(k + 2)
    parts = mxu(near, near_high[k], NT) + mxu(near, near_low[k], NT)
    parts = parts + mxu(jnp.concatenate([far, far], axis=1), above[k], NN)
    ex[pl.ds(pl.multiple_of(8 * k, 8), 8), :] = fold(parts)


def get_ex(ex):
    return [ex[pl.ds(comp, ex.shape[0] // 8, stride=8), :] for comp in range(3)]


def main_kernel(
    n_head, n_track,
    pot_hbm, src_hbm, dk_hbm, mag_hbm, foot_hbm, temp_hbm, prof_hbm, self_hbm, next_hbm,
    pot, near_high, near_low, above, lhs, ex, rim_new, state_out, applied_out, target_out,
    mid, src, faces, dk, mag, foot, tidx, prof, tself, tnext,
    rim, edge, edge_new, lines, lines_in, lines_mid, lines_mid_in,
    addr, ask, asked, surf, answer, answered,
    in_sem, halo_send, halo_recv, mid_send, mid_recv, rim_send, rim_recv,
    rim_new_send, rim_new_recv, ask_send, ask_recv, ans_send, ans_recv,
):
    head, track, has_low_x, has_high_x, has_low_y, has_high_y = has_neighbours(n_head, n_track)
    n_x, n_y, n_z = src.shape
    n_tiles, width = mag.shape[1:]
    inner, all_x = pl.ds(ROW0, n_y), pl.ds(1, n_x)
    low_x, high_x = (head - 1, track), (head + 1, track)
    low_y, high_y = (head, track - 1), (head, track + 1)
    rows8 = lax.broadcasted_iota(I32, (8, 128), 0)

    barrier, n_greeted = greet(n_head, n_track)
    part = n_x // PARTS
    parts = range(0, n_x, part)
    pairs = [
        (foot_hbm, foot),
        (mag_hbm, mag),
        (pot_hbm.at[:, pl.ds(0, 1), :], lines.at[0]),
        (pot_hbm.at[:, pl.ds(n_y - 1, 1), :], lines.at[1]),
        *[(pot_hbm.at[pl.ds(x, part), :, :], pot.at[pl.ds(x + 1, part), inner, :]) for x in parts],
        *[(src_hbm.at[pl.ds(x, part), :, :], src.at[pl.ds(x, part), :, :]) for x in parts],
        (dk_hbm, dk),
        (temp_hbm, tidx),
        (prof_hbm, prof),
        (self_hbm, tself),
        (next_hbm, tnext),
    ]
    loads = [pltpu.make_async_copy(a, b, in_sem.at[i]) for i, (a, b) in enumerate(pairs)]
    large = loads[4 : 4 + 2 * PARTS]
    small = loads[4 + 2 * PARTS : -2]
    for copy in loads[:-2]:
        copy.start()

    for side, there in enumerate((has_low_x, has_high_x)):

        @pl.when(jnp.logical_not(there))
        def _():
            for ref in (pot, mid):
                ref[side * (n_x + 1), ROW0 : ROW0 + n_y, :] = jnp.zeros((n_y, n_z), F32)
            for ref in (rim, rim_new):
                ref[side] = jnp.zeros(ref.shape[1:], F32)

    for side, there in enumerate((has_low_y, has_high_y)):

        @pl.when(jnp.logical_not(there))
        def _():
            for ref in (lines_in, lines_mid_in):
                ref[side] = jnp.zeros(ref.shape[1:], F32)

    loads[0].wait()
    rank_grains(foot, addr, ask, n_track)
    asked[track] = ask[track]
    loads[1].wait()
    put_edges(edge, [[mag[comp] for comp in range(3)]] * 2)
    loads[2].wait()
    loads[3].wait()
    pl.semaphore_wait(barrier, n_greeted)

    def halo(planes, rows, target, rows_in, send, recv):
        return [
            (has_low_x, remote(planes[0], target.at[n_x + 1, inner, :], send.at[0], recv.at[1], low_x)),
            (has_high_x, remote(planes[1], target.at[0, inner, :], send.at[1], recv.at[0], high_x)),
            (has_low_y, remote(rows.at[0], rows_in.at[1], send.at[2], recv.at[3], low_y)),
            (has_high_y, remote(rows.at[1], rows_in.at[0], send.at[3], recv.at[2], high_y)),
        ]

    def halo_waits(planes, rows, target, rows_in, send, recv):
        return [
            (has_low_x, remote(planes[0], target.at[0, inner, :], send.at[0], recv.at[0], low_x)),
            (has_high_x, remote(planes[1], target.at[n_x + 1, inner, :], send.at[1], recv.at[1], high_x)),
            (has_low_y, remote(rows.at[0], rows_in.at[0], send.at[2], recv.at[2], low_y)),
            (has_high_y, remote(rows.at[1], rows_in.at[1], send.at[3], recv.at[3], high_y)),
        ]

    def place_lines(rows_in, target):
        target[1 : n_x + 1, ROW0 - 1 : ROW0, :] = rows_in[0]
        target[1 : n_x + 1, ROW0 + n_y : ROW0 + n_y + 1, :] = rows_in[1]

    everyone = pl.ds(0, n_track - 1)
    next_one = (head, lax.rem(track + 1, n_track))
    all_asks = remote(ask.at[everyone], asked.at[everyone], ask_send, ask_recv, next_one)
    all_answers = remote(answer.at[everyone], answered.at[everyone], ans_send, ans_recv, next_one)

    start_halo = [pot_hbm.at[0], pot_hbm.at[n_x - 1]], lines, pot, lines_in, halo_send, halo_recv
    start(halo(*start_halo))

    def send_ask(step, _):
        other = lax.rem(track + step, n_track)
        remote(ask.at[other], asked.at[track], ask_send, ask_recv, (head, other)).start()
        return 0

    lax.fori_loop(1, n_track, send_ask, 0)
    start(rim_copies(n_head, n_track, edge, rim, rim_send, rim_recv, False))
    for copy in large:
        copy.wait()
    for copy in loads[-2:]:
        copy.start()

    edge_rows = 32

    def sweep_chunk(source, target, row, rows_at, unroll, beside=None):
        rows = slice(ROW0 + row, ROW0 + row + rows_at)

        def planes(base, count, carried):
            for j in range(count):
                target[base + j + 1, rows, :], carried = swept(source, src, faces, j, base + j, row, rows_at, carried)
            return carried

        def trip(i, carried):
            if beside is not None:
                beside(i)
            return planes(1 + unroll * i, unroll, carried)

        trips = (n_x - 2) // unroll
        carried = planes(1, unroll, face(source[1, rows, :], source[2, rows, :]))
        carried = lax.fori_loop(1, trips, trip, carried)
        if beside is not None:
            beside(trips)
        planes(1 + unroll * trips, n_x - 2 - unroll * trips, carried)

    def sweep_inner(source, target):
        sweep_chunk(source, target, edge_rows, n_y - 2 * edge_rows, 8)

    def sweep_outer(source, target):
        for side, x in enumerate((0, n_x - 1)):
            for row in range(0, n_y, edge_rows):
                rows = slice(ROW0 + row, ROW0 + row + edge_rows)
                carried = face(source[x, rows, :], source[x + 1, rows, :])
                slot = 4 * side + row // edge_rows
                target[x + 1, rows, :], _ = swept(source, src, faces, slot, x, row, edge_rows, carried)

    def sweep_edge(source, target, row, beside=None):
        sweep_chunk(source, target, row, edge_rows, 8 if beside else 16, beside)

    sweep_inner(pot, mid)
    finish(halo_waits(*start_halo), False)
    place_lines(lines_in, pot)
    sweep_outer(pot, mid)
    mid_halo = [mid.at[1, inner, :], mid.at[n_x, inner, :]], lines_mid, mid, lines_mid_in, mid_send, mid_recv
    sends = halo(*mid_halo)
    start(sends[:2])
    sweep_edge(pot, mid, 0)
    lines_mid[0] = mid[1 : n_x + 1, ROW0 : ROW0 + 1, :]
    start(sends[2:3])
    sweep_edge(pot, mid, n_y - edge_rows)
    lines_mid[1] = mid[1 : n_x + 1, ROW0 + n_y - 1 : ROW0 + n_y, :]
    start(sends[3:])

    sweep_inner(mid, pot)
    small[0].wait()
    kernels = []
    for odd in range(2):
        weights = jnp.zeros((8, 128), F32)
        for comp in range(3):
            weights = weights + jnp.where(
                rows8 == 2 * comp + odd, jnp.broadcast_to(dk[comp : comp + 1, :], (8, 128)), 0.0
            )
        high = weights.astype(BF16).astype(F32)
        kernels.append(jnp.concatenate([high, weights - high], axis=0))
    kernels = jnp.concatenate(kernels, axis=0).astype(BF16)
    kernels = jnp.concatenate([kernels, kernels], axis=1)

    def surface(i):
        for j in range(4):
            at = 4 * (i - 1) + j
            both = [halves(pot[2 * at + odd + 1, ROW0 : ROW0 + n_y, :]) for odd in range(2)]
            found = mxu(kernels, jnp.concatenate(both, axis=0), NT)
            total = (found[0:8, :n_y] + found[8:16, :n_y]) + (found[16:24, n_y:] + found[24:32, n_y:])
            surf[pl.ds(8 * at if isinstance(at, int) else pl.multiple_of(8 * at, 8), 8), :] = total

    finish(halo_waits(*mid_halo), False)
    place_lines(lines_mid_in, mid)
    sweep_outer(mid, pot)
    sweep_edge(mid, pot, 0)
    sweep_edge(mid, pot, n_y - edge_rows, surface)
    surface(n_x // 8)

    all_asks.wait_recv()
    table = halves(surf[...])

    def reply(far_y, own):
        y, z, x = track // 8, (track // 4) % 2, track % 4
        others = [
            (y + far_y) % 4 * 8 + (z + far_z) % 2 * 4 + (x + far_x) % 4
            for far_z in (1, 0)
            for far_x in (2, 1, 3, 0)
        ]
        for other in others:
            low, high = lookup(table, [asked[other, 0:1, :], asked[other, 1:2, :]])
            answer[other] = jnp.where(rows8 % 2 == 0, low, pltpu.roll(high, 1, 0))
        if own:
            answered[track] = answer[track]
            others = others[:-1]
        for other in others:
            remote(answer.at[other], answered.at[track], ans_send, ans_recv, (head, other)).start()

    def reply_far(group, _):
        reply(jnp.where(group == 0, 2, jnp.where(group == 1, 1, 3)), False)
        return 0

    lax.fori_loop(0, 3, reply_far, 0)
    reply(0, True)

    def set_lhs(tile, value, comp):
        high = value.astype(BF16).astype(F32)
        lhs[pl.ds(16 * tile + comp, value.shape[0], stride=16), :] = high
        lhs[pl.ds(16 * tile + 8 + comp, value.shape[0], stride=16), :] = value - high

    lhs[...] = jnp.zeros(lhs.shape, F32)
    finish(rim_copies(n_head, n_track, edge, rim, rim_send, rim_recv, True), False)
    for side, tile in ((0, 0), (1, n_tiles + 1)):
        high = rim[side].astype(BF16).astype(F32)
        lhs[16 * tile : 16 * tile + 8, :] = high
        lhs[16 * tile + 8 : 16 * tile + 16, :] = rim[side] - high
    state = [mag[comp] for comp in range(3)]
    for comp in range(3):
        set_lhs(1, state[comp], comp)
    for copy in [*small[1:], *loads[-2:]]:
        copy.wait()

    def first_exchange(k, _):
        self_high, self_low = split(tself[k])
        next_high, next_low = split(tnext[k])
        near_high[k] = jnp.concatenate([self_high, next_high], axis=1)
        near_low[k] = jnp.concatenate([self_low, next_low], axis=1)
        above[k] = jnp.concatenate([next_high, next_low], axis=0)
        exchange(k, lhs, near_high, near_low, above, ex)
        return 0

    def next_exchange(k, _):
        exchange(k, lhs, near_high, near_low, above, ex)
        return 0

    lax.fori_loop(0, n_tiles, first_exchange, 0, unroll=4)
    profile = jnp.broadcast_to(prof[...], (8, 128))
    temp = jnp.concatenate(
        [jnp.take_along_axis(profile, tidx[at : at + 8, :], axis=1) for at in range(0, n_tiles, 8)], axis=0
    )
    target = 0.05 + jnp.maximum(1.0 - temp, 0.0)

    all_answers.wait_recv()
    table = halves(answered[...].reshape(8 * n_track, 128))
    applied = [[None] * n_tiles for _ in range(3)]

    def find(pair):
        found = lookup(table, [addr[2 * pair + i : 2 * pair + i + 1, :] for i in range(2)])
        for i, value in enumerate(found):
            for comp in range(3):
                applied[comp][2 * pair + i] = value[2 * comp : 2 * comp + 1, :]

    last_pair = n_tiles // 2 - 1
    find(0)
    find(last_pair)
    exs = get_ex(ex)
    blank = jnp.zeros((6, width), F32)
    sides = []
    for rows, order in ((slice(0, 8), (0, 1, None)), (slice(n_tiles - 8, n_tiles), (None, n_tiles - 2, n_tiles - 1))):
        fields = [
            jnp.concatenate([blank if at is None else applied[comp][at] for at in order], axis=0) + exs[comp][rows]
            for comp in range(3)
        ]
        sides.append(llb_section([m[rows] for m in state], fields, target[rows]))
    put_edges(edge_new, sides)
    start(rim_copies(n_head, n_track, edge_new, rim_new, rim_new_send, rim_new_recv, False))
    for pair in range(1, last_pair):
        find(pair)
    applied = [jnp.concatenate(rows, axis=0) for rows in applied]
    state = llb_section(state, [a + e for a, e in zip(applied, exs)], target)
    for comp in range(3):
        state_out[comp] = state[comp]
        applied_out[comp] = applied[comp]
    target_out[...] = target

    lhs[0:16, :] = jnp.zeros((16, width), F32)
    lhs[16 * (n_tiles + 1) :, :] = jnp.zeros((16, width), F32)
    for comp in range(3):
        set_lhs(1, state[comp], comp)
    lax.fori_loop(0, EARLY, next_exchange, 0, unroll=4)

    all_asks.wait_send()
    all_answers.wait_send()
    finish(halo_waits(*start_halo), True)
    finish(halo_waits(*mid_halo), True)
    finish(rim_copies(n_head, n_track, edge, rim, rim_send, rim_recv, True), True)
    new_rim = rim_copies(n_head, n_track, edge_new, rim_new, rim_new_send, rim_new_recv, True)
    finish(new_rim, True)
    finish(new_rim, False)


def last_kernel(
    pot, near_high, near_low, above, lhs, ex_early, rim_new, state_in, applied, target,
    relaxed_hbm, magnet_hbm,
    ex, state_out, sem,
):
    n_x, n_y, _ = relaxed_hbm.shape
    n_tiles, width = target.shape
    part = n_x // PARTS
    stores = [
        pltpu.make_async_copy(
            pot.at[pl.ds(part * i + 1, part), pl.ds(ROW0, n_y), :], relaxed_hbm.at[pl.ds(part * i, part), :, :], sem.at[i]
        )
        for i in range(PARTS)
    ]
    for store in stores:
        store.start()
    ex[0 : 8 * EARLY, :] = ex_early[0 : 8 * EARLY, :]

    def next_exchange(k, _):
        exchange(k, lhs, near_high, near_low, above, ex)
        return 0

    lax.fori_loop(EARLY, n_tiles, next_exchange, 0, unroll=4)
    for side, tile in ((0, 0), (1, n_tiles - 1)):
        high = rim_new[side].astype(BF16).astype(F32)
        both = jnp.concatenate([high, rim_new[side] - high], axis=0).astype(BF16)
        if side == 0:
            parts = mxu(both, near_high[tile][:, width:], NT) + mxu(both, near_low[tile][:, width:], NT)
        else:
            parts = mxu(jnp.concatenate([both, both], axis=1), above[tile], NN)
        ex[8 * tile : 8 * tile + 8, :] = ex[8 * tile : 8 * tile + 8, :] + fold(parts)
    state = [state_in[comp] for comp in range(3)]
    fields = [applied[comp] + e for comp, e in enumerate(get_ex(ex))]
    for comp, value in enumerate(llb_section(state, fields, target[...])):
        state_out[comp] = value
    copy = pltpu.make_async_copy(state_out, magnet_hbm, sem.at[PARTS])
    copy.start()
    copy.wait()
    for store in stores:
        store.wait()


def per_device(n_head, n_track, potential, source, depth_kernel, magnet, footprint, temp_index, temp_profile, self_tiles, next_tiles):
    n_x, n_y, n_z = potential.shape
    n_tiles, width = self_tiles.shape[1], self_tiles.shape[2]
    padded = (n_x + 2, n_y + 16, n_z)
    hbm, vmem, dma = pltpu.HBM, pltpu.VMEM, pltpu.SemaphoreType.DMA
    in_hbm = pl.BlockSpec(memory_space=hbm)
    in_vmem = pl.BlockSpec(memory_space=vmem)
    arguments = (
        potential,
        source,
        depth_kernel,
        magnet.reshape(3, n_tiles, width),
        footprint.reshape(n_tiles, width),
        temp_index.reshape(n_tiles, width),
        temp_profile.reshape(1, -1),
        self_tiles[0],
        next_tiles[0],
    )
    arguments = [pltpu.with_memory_space_constraint(a, hbm) for a in arguments]
    grains = (3, n_tiles, width)
    shared = (
        vmem(padded, F32),
        vmem((n_tiles, width, 2 * width), BF16),
        vmem((n_tiles, width, 2 * width), BF16),
        vmem((n_tiles, 2 * width, width), BF16),
        vmem((16 * (n_tiles + 2), width), F32),
        vmem((8 * n_tiles, width), F32),
        vmem((2, 8, width), F32),
        vmem(grains, F32),
        vmem(grains, F32),
        vmem((n_tiles, width), F32),
    )
    results = pl.pallas_call(
        functools.partial(main_kernel, n_head, n_track),
        out_shape=shared,
        in_specs=[in_hbm] * 9,
        out_specs=(in_vmem,) * len(shared),
        scratch_shapes=[
            vmem(padded, F32),
            vmem((n_x, n_y, n_z), F32),
            vmem((2, 16, n_y, n_z), F32),
            vmem((3, n_z), F32),
            vmem(grains, F32),
            vmem((n_tiles, width), I32),
            vmem((n_tiles, width), I32),
            vmem((1, 128), F32),
            vmem((n_tiles, width, width), F32),
            vmem((n_tiles, width, width), F32),
            *[vmem((2, 8, width), F32)] * 3,
            *[vmem((2, n_x, 1, n_z), F32)] * 4,
            vmem((n_tiles, width), I32),
            vmem((n_track, 2, width), I32),
            vmem((n_track, 2, width), I32),
            vmem((8 * (n_x // 2), n_y), F32),
            vmem((n_track, 8, width), F32),
            vmem((n_track, 8, width), F32),
            dma((9 + 2 * PARTS,)),
            *[dma((4,))] * 4,
            *[dma((2,))] * 4,
            *[dma] * 4,
        ],
        compiler_params=pltpu.CompilerParams(
            collective_id=0, has_side_effects=True, vmem_limit_bytes=24 << 20
        ),
        name="pole_and_grains",
    )(*arguments)
    relaxed, magnet_out = pl.pallas_call(
        last_kernel,
        out_shape=(hbm(potential.shape, F32), hbm(grains, F32)),
        in_specs=[in_vmem] * len(shared),
        out_specs=(in_hbm, in_hbm),
        scratch_shapes=[vmem((8 * n_tiles, width), F32), vmem(grains, F32), dma((PARTS + 1,))],
        compiler_params=pltpu.CompilerParams(vmem_limit_bytes=4 << 20),
        name="results",
    )(*results)
    return relaxed, magnet_out.reshape(magnet.shape)


def solution(mesh):
    in_specs = (
        P("head", "track", None),
        P("head", "track", None),
        P(),
        P(None, "track", "head"),
        P("track", "head"),
        P("track", "head"),
        P(),
        P("track", "head", None, None),
        P("track", "head", None, None),
    )
    out_specs = (P("head", "track", None), P(None, "track", "head"))
    return jax.shard_map(
        functools.partial(per_device, mesh.shape["head"], mesh.shape["track"]),
        mesh=mesh,
        in_specs=in_specs,
        out_specs=out_specs,
        check_vma=False,
    )
```
